32 devices in a mesh: region: 8 (over z, y), member: 4 (over x, core).
Axes of the slice: x: 2, y: 2, z: 4, core: 2. Of those that a mesh axis runs over, the one named last changes fastest.
Arguments:
- ensemble: bfloat16 [256, 16384], P('member', 'region'), may hold values from -6 to 6
- reports: float32 [8, 1024], P('region'), may hold values from -6 to 6
- report_count: int32 [8], P('region'), may hold values from 128 to 1024, as said below
- report_cell: int32 [8, 1024], P('region'), may hold values from 0 to 16383, as said below
- report_weight: float32 [8, 16, 1024], P('region', 'member'), may hold values from 0.001 to 1
- blending: float32 [4, 16384], P(None, ('region', 'member')), may hold values from 0.02 to 1
Outputs:
- analysis: bfloat16 [16384, 256], P(('region', 'member'))
The draws below stay inside these ranges and needn't reach their ends.
Inputs may be any that keep to these rules, and one draw needn't show every extreme that they name: `report_count`: the largest value 1024 is reached by some region in every draw. `report_cell`: every cell lies in the slot's own region, or in the first 128 cells of one of at most two other regions chosen for that region.
All inputs are finite; a program needn't handle non-finite values.
Results may differ from the reference program's by a relative error of at most 0.0055.
Values may be sent and summed in bfloat16 or wider, within the bound.
No kernel may reach another device: no remote copies, remote signals or barrier semaphores. Data moves between devices by JAX's collectives and lax.ppermute only.
A program may use at most 64 MiB of HBM per device.

```python
import math
import jax
import jax.numpy as jnp
from jax import lax

MEMBERS = 256
REPORTS = 1024
POINTS_DEV = 4
MARGIN = 128
SWEEPS = 4
REGIONS = 8
POINT_ROWS = 4
POINTS = 16
CELLS = 2048
ALL_CELLS = 16384


def draw_report_count(key, part):
    counts = jax.random.randint(key, (REGIONS,), REPORTS // 8, REPORTS + 1)
    fullest = jax.random.randint(jax.random.fold_in(key, 7), (), 0, REGIONS)
    return jnp.where(jnp.arange(REGIONS) == fullest, REPORTS, counts).astype(jnp.int32)


def draw_report_cell(key, part):
    streams = jax.random.split(jax.random.fold_in(key, 11), 5)
    first_pick = jax.random.randint(streams[0], (REGIONS,), 0, REGIONS - 1)
    second_pick = jax.random.randint(streams[1], (REGIONS,), 0, REGIONS - 2)
    region = jnp.arange(REGIONS)
    source_one = (region + 1 + first_pick) % REGIONS
    source_two = (region + 1 + (first_pick + 1 + second_pick) % (REGIONS - 1)) % REGIONS
    kinds = jax.random.randint(streams[2], (REGIONS, REPORTS), 0, 4)
    home_cell = jax.random.randint(streams[3], (REGIONS, REPORTS), 0, CELLS)
    edge_cell = jax.random.randint(streams[4], (REGIONS, REPORTS), 0, MARGIN)
    holder = jnp.where(kinds == 2, source_one[:, None], jnp.where(kinds == 3, source_two[:, None], region[:, None]))
    placed = jnp.where(kinds >= 2, edge_cell, home_cell)
    result = holder * CELLS + placed
    position = jnp.arange(REPORTS)[None, :]
    result = jnp.where((region[:, None] == REGIONS - 1) & (position == 0), REGIONS * CELLS - 1, result)
    result = jnp.where((region[:, None] == 0) & (position == 0), 0, result)
    return result.astype(jnp.int32)


def block_levels(stream_key, extent, shards, low, top_value):
    gain = 1.0
    for dim, blocks in shards:
        draws = jax.random.uniform(jax.random.fold_in(jax.random.fold_in(stream_key, 6), dim), (blocks,), jnp.float32, low / len(shards), top_value / len(shards))
        gain = gain * jnp.repeat(jnp.exp(draws), extent[dim] // blocks).reshape((-1,) + (1,) * (len(extent) - 1 - dim))
    return gain


def scatter_about(own_key, extent, scale, limit, pieces=(), kind=jnp.bfloat16):
    drawn = scale * jax.random.normal(own_key, extent, jnp.float32)
    if pieces:
        drawn = drawn * block_levels(own_key, extent, pieces, -0.22, 0.18)
    return jnp.clip(drawn, -limit, limit).astype(kind)


def setup_inputs(seed: int = 0) -> dict:
    arg_keys = jax.random.split(jax.random.key(seed), 7)
    ensemble = scatter_about(arg_keys[0], (MEMBERS, ALL_CELLS), 1.0, 6.0, ((0, 4), (1, 8)))
    reports = scatter_about(arg_keys[1], (REGIONS, REPORTS), 1.0, 6.0, ((0, 8),), jnp.float32)
    report_count = draw_report_count(jax.random.fold_in(arg_keys[6], 71), 0)
    report_cell = draw_report_cell(jax.random.fold_in(arg_keys[6], 71), 0)
    report_weight = jnp.clip(jnp.exp(math.log(1.0) - 6.9077552 * jax.random.uniform(arg_keys[4], (REGIONS, POINTS, REPORTS), jnp.float32) ** block_levels(arg_keys[4], (REGIONS, POINTS, REPORTS), ((0, 8), (1, 4)), -0.2, 0.2)), 0.001, 1.0)
    blending = jnp.clip(jnp.exp(math.log(1.0) - 3.912023 * jax.random.uniform(arg_keys[5], (4, ALL_CELLS), jnp.float32) ** block_levels(arg_keys[5], (4, ALL_CELLS), ((1, 32),), -0.2, 0.2)), 0.02, 1.0)
    return dict(ensemble=ensemble, reports=reports, report_count=report_count, report_cell=report_cell, report_weight=report_weight, blending=blending)


highest = lax.Precision.HIGHEST

def make_transform(products, forcing, members):
    identity = jnp.eye(members, dtype=jnp.float32)
    precision_mat = (members - 1.0) * identity[None] + products
    frobenius = jnp.sqrt(lax.optimization_barrier(jnp.sum(precision_mat * precision_mat, axis=(1, 2))))
    current = precision_mat / frobenius[:, None, None]
    root_iter = jnp.broadcast_to(identity, current.shape)
    for iteration in range(SWEEPS):
        middle = 1.5 * identity[None] - 0.5 * jnp.einsum('aij,ajk->aik', root_iter, current, precision=highest)
        current = jnp.einsum('aij,ajk->aik', current, middle, precision=highest)
        root_iter = jnp.einsum('aij,ajk->aik', middle, root_iter, precision=highest)
    inverse_root = root_iter / jnp.sqrt(frobenius)[:, None, None]
    inner_step = jnp.einsum('aij,aj->ai', inverse_root, forcing, precision=highest)
    mean_weights = jnp.einsum('aij,aj->ai', inverse_root, inner_step, precision=highest)
    return (mean_weights[:, :, None] + jnp.sqrt(members - 1.0) * inverse_root).astype(jnp.bfloat16)

def corner_layout(band_index, points_here, row_count):
    group_index = jnp.arange(4 * points_here, dtype=jnp.int32)
    upper_half = group_index // (2 * points_here)
    column_block = group_index // 2 % points_here
    right_half = group_index % 2
    row_base = jnp.clip(band_index - 1 + upper_half, 0, row_count - 2)
    col_base = jnp.clip(column_block - 1 + right_half, 0, points_here - 2)
    return (row_base, col_base)

def reference(ensemble, reports, report_count, report_cell, report_weight, blending):
    members = ensemble.shape[0]
    regions = reports.shape[0]
    cell_count = ensemble.shape[1] // regions
    groups_band = 4 * POINTS_DEV
    group_cells = cell_count // (POINT_ROWS * groups_band)
    mixing_all = blending / lax.optimization_barrier(jnp.sum(blending, axis=0, keepdims=True))
    bands = jnp.arange(POINT_ROWS, dtype=jnp.int32)[:, None]
    row_base, col_base = corner_layout(bands, POINTS_DEV, POINT_ROWS)

    def per_region(region):
        at_reports = jnp.take(ensemble, report_cell[region], axis=1).astype(jnp.float32)
        report_mean = lax.optimization_barrier(jnp.sum(at_reports, axis=0)) / members
        report_pert = (at_reports - report_mean[None, :]).astype(jnp.bfloat16)
        active = (jnp.arange(report_pert.shape[1]) < report_count[region]).astype(jnp.float32)
        weights = report_weight[region] * active[None, :]
        weighted = (report_pert.astype(jnp.float32)[None, :, :] * weights[:, None, :]).astype(jnp.bfloat16)
        departure = (weights * (reports[region] - report_mean)[None, :]).astype(jnp.bfloat16)
        products = jnp.einsum('ako,jo->akj', weighted.astype(jnp.float32), report_pert.astype(jnp.float32), precision=highest)
        forcing = jnp.einsum('ao,ko->ak', departure.astype(jnp.float32), report_pert.astype(jnp.float32), precision=highest)
        transform = make_transform(products, forcing, members)
        block_cells = lax.dynamic_slice_in_dim(ensemble, region * cell_count, cell_count, 1).astype(jnp.float32)
        cell_mean = lax.optimization_barrier(jnp.sum(block_cells, axis=0)) / members
        anomaly = (block_cells - cell_mean[None, :]).astype(jnp.bfloat16)
        anomaly_view = anomaly.astype(jnp.float32).reshape(members, POINT_ROWS, groups_band, group_cells)
        mixing = lax.dynamic_slice_in_dim(mixing_all, region * cell_count, cell_count, 1)
        mixing = mixing.reshape(4, POINT_ROWS, groups_band, group_cells)
        blended = jnp.zeros((POINT_ROWS, groups_band, group_cells, members), jnp.float32)
        for corner in range(4):
            row_step = corner // 2
            col_step = corner % 2
            chosen_index = ((row_base + row_step) * POINTS_DEV + col_base + col_step).reshape(-1)
            chosen = jnp.take(transform, chosen_index, axis=0).astype(jnp.float32)
            chosen = chosen.reshape(POINT_ROWS, groups_band, members, members)
            spread = jnp.einsum('kngc,ngkj->ngcj', anomaly_view, chosen, precision=highest)
            blended = blended + mixing[corner][..., None] * spread
        blended = blended.reshape(cell_count, members)
        return (cell_mean[:, None] + blended).astype(jnp.bfloat16)
    result = lax.map(per_region, jnp.arange(regions, dtype=jnp.int32))
    return result.reshape(regions * cell_count, members)
```

```python
import functools

import jax
import jax.numpy as jnp
from jax import lax
from jax.experimental import pallas as pl
from jax.experimental.pallas import tpu as pltpu
from jax.sharding import PartitionSpec as P

MARGIN = 128
LANES = 128
AXES = ("region", "member")

f32 = jnp.float32
bf16 = jnp.bfloat16

VMEM = pl.BlockSpec(memory_space=pltpu.VMEM)
SMEM = pl.BlockSpec(memory_space=pltpu.SMEM)


def dot_nn(a, b):
    return lax.dot_general(a, b, (((1,), (0,)), ((), ())), preferred_element_type=f32)


def dot_nt(a, b):
    return lax.dot_general(a, b, (((1,), (1,)), ((), ())), preferred_element_type=f32)


def split(x):
    high = x.astype(bf16)
    return high, (x - high.astype(f32)).astype(bf16)


def call(kernel, outs, smem_count, inputs, flops, moved, scratch=()):
    return pl.pallas_call(
        kernel,
        out_shape=[jax.ShapeDtypeStruct(s, d) for s, d in outs],
        in_specs=[SMEM] * smem_count + [VMEM] * (len(inputs) - smem_count),
        out_specs=[VMEM] * len(outs),
        scratch_shapes=list(scratch),
        cost_estimate=pl.CostEstimate(flops=flops, bytes_accessed=moved, transcendentals=0),
    )(*inputs)


def weights_kernel(rows, numbers, cell_ref, weight_ref, report_ref, out_ref):
    cell = cell_ref[...]
    points, slots = weight_ref.shape[1:]
    count = numbers[4]
    holder = cell // count
    within = cell - holder * count
    low = within % LANES
    high = jnp.where(
        holder == numbers[0],
        within // LANES,
        jnp.where(holder == numbers[1], rows - 2, rows - 1),
    )
    active = lax.broadcasted_iota(jnp.int32, (1, slots), 1) < numbers[3]
    weights = jnp.where(active, weight_ref[0], 0.0)
    values = jnp.concatenate([weights, weights * report_ref[...]], axis=0)
    low_hot = (lax.broadcasted_iota(jnp.int32, (LANES, slots), 0) == low).astype(f32).astype(bf16)
    chosen = jnp.concatenate(
        [jnp.where(high == row, values, 0.0) for row in range(rows)], axis=0
    )
    first, second = split(chosen)
    total = dot_nt(first, low_hot) + dot_nt(second, low_hot)
    out_ref[...] = total.reshape(rows, 2 * points, LANES)


def anomaly_kernel(offsets, numbers, *refs):
    pieces, (anomaly_ref, mean_ref) = refs[:-2], refs[-2:]
    rows = pieces[0].shape[0]
    members = rows * len(pieces)
    total = jnp.sum(pieces[0][...].astype(f32), axis=0, keepdims=True)
    for piece in pieces[1:]:
        total = total + jnp.sum(piece[...].astype(f32), axis=0, keepdims=True)
    mean = total / members
    mean_ref[...] = mean
    for offset, piece in zip(offsets, pieces):
        start = pl.multiple_of((numbers[0] ^ offset) * rows, rows)
        anomaly_ref[pl.ds(start, rows), :] = (piece[...].astype(f32) - mean).astype(bf16)


def products_kernel(anomaly_ref, mean_ref, table_ref, products_ref, forcing_ref):
    members, cells = anomaly_ref.shape
    points = products_ref.shape[0]
    chunk = min(cells, 2048)
    forcing = None
    for start in range(0, cells, chunk):
        block = anomaly_ref[:, start : start + chunk]
        departures = []
        for a in range(points):
            scaled = []
            for h in range(start // LANES, (start + chunk) // LANES):
                lanes = slice(h * LANES, (h + 1) * LANES)
                scaled.append(
                    (anomaly_ref[:, lanes].astype(f32) * table_ref[h, a : a + 1, :]).astype(bf16)
                )
            part = dot_nt(jnp.concatenate(scaled, axis=1), block)
            if start == 0:
                products_ref[a] = part
            else:
                products_ref[a] += part
        for h in range(start // LANES, (start + chunk) // LANES):
            lanes = slice(h * LANES, (h + 1) * LANES)
            tile = table_ref[h]
            departures.append(tile[points:, :] - tile[:points, :] * mean_ref[:, lanes])
        departure = jnp.concatenate(departures, axis=1)
        first, second = split(jnp.concatenate([departure, departure], axis=0))
        part = dot_nt(first, block) + dot_nt(second, block)
        forcing = part if forcing is None else forcing + part
    forcing_ref[...] = forcing


def transpose_kernel(numbers, anomaly_ref, mean_ref, own_ref, first_ref, second_ref, column_ref):
    members = anomaly_ref.shape[0]
    slab = own_ref.shape[0]
    half = second_ref.shape[0]
    for ref, start in ((own_ref, numbers[0]), (first_ref, numbers[1])):
        for u in range(2):
            part = anomaly_ref[:, pl.ds(pl.multiple_of(start + u * half, half), half)]
            ref[u * half : (u + 1) * half, :] = part.T
    part = anomaly_ref[:, pl.ds(pl.multiple_of(numbers[2], half), half)]
    second_ref[...] = part.T
    row = mean_ref[:, pl.ds(pl.multiple_of(numbers[0], half), slab)]
    column_ref[...] = jnp.broadcast_to(row, (8, slab)).T


def column_bases(points):
    return [min(max(b - 1 + v, 0), points - 2) for b in range(points) for v in range(2)]


def blended_parts(segments, transforms, points):
    half = segments[0][0].shape[0]
    bases = column_bases(points)
    size = half // len(bases)
    spans = []
    for v in range(points - 1):
        hits = [g for g, b in enumerate(bases) if b == v]
        spans.append((hits[0] * size, (hits[-1] + 1) * size))
    sums = [[None] * (points - 1) for _ in segments]
    for q in range(points):
        where = [v for v in (q - 1, q) if 0 <= v <= points - 2]
        rows = [
            (n, v, cells[spans[v][0] : spans[v][1], :])
            for n, (cells, _) in enumerate(segments)
            for v in where
        ]
        spread = dot_nn(jnp.concatenate([r[2] for r in rows], axis=0), transforms(q))
        at = 0
        for n, v, cells in rows:
            low, high = spans[v]
            term = segments[n][1][low:high, q : q + 1] * spread[at : at + high - low]
            sums[n][v] = term if sums[n][v] is None else sums[n][v] + term
            at += high - low
    return [jnp.concatenate(parts, axis=0) for parts in sums]


def transform_kernel(
    offsets, numbers, *refs
):
    count = len(offsets)
    pieces = refs[:count]
    (
        table_ref,
        products_ref,
        forcing_ref,
        first_ref,
        second_ref,
        first_mix,
        second_mix,
        transform_ref,
        to_first_ref,
        to_second_ref,
        margin_ref,
    ) = refs[count:]
    rows = pieces[0].shape[1]
    members = rows * count
    points = products_ref.shape[0]
    for offset, piece in zip(offsets, pieces):
        for j in range(2):
            start = pl.multiple_of((numbers[0] ^ offset ^ numbers[1 + j]) * rows, rows)
            margin_ref[pl.ds(start, rows), j * LANES : (j + 1) * LANES] = piece[j]
    values = margin_ref[...].astype(f32)
    mean = jnp.sum(values, axis=0, keepdims=True) / members
    pert = (values - mean).astype(bf16)
    pert_wide = pert.astype(f32)
    tiles = jnp.concatenate([table_ref[0], table_ref[1]], axis=1)
    departure = tiles[points:, :] - tiles[:points, :] * mean
    first, second = split(jnp.concatenate([departure, departure], axis=0))
    forcing = forcing_ref[...] + dot_nt(first, pert) + dot_nt(second, pert)
    forcing = forcing.T
    identity = lax.broadcasted_iota(jnp.int32, (members, members), 0) == lax.broadcasted_iota(
        jnp.int32, (members, members), 1
    )

    def plus(scalar, matrix):
        return matrix + jnp.where(identity, scalar, 0.0)

    def left(x):
        high, low = split(x)
        return jnp.concatenate([high, high, low], axis=1)

    def right(x):
        high, low = split(x)
        return jnp.concatenate([high, low, high], axis=0)

    span = range(points)
    matrix, scale = [], []
    for a in span:
        weighted = (pert_wide * tiles[a : a + 1, :]).astype(bf16)
        full = plus(members - 1.0, products_ref[a] + dot_nt(weighted, pert))
        square = jnp.sum(jnp.sum(full * full, axis=0, keepdims=True), axis=1, keepdims=True)
        frobenius = jnp.sqrt(square)
        matrix.append(full / frobenius)
        scale.append(1.0 / jnp.sqrt(frobenius))
    matrix_left = [left(x) for x in matrix]
    squared = [dot_nn(matrix_left[a], right(matrix[a])) for a in span]
    root = [
        plus(2.25, -2.4375 * matrix[a])
        + dot_nn(
            left(squared[a]),
            right(plus(1.6875, 0.0625 * squared[a] - 0.5625 * matrix[a])),
        )
        for a in span
    ]
    current = [dot_nn(matrix_left[a], right(root[a])) for a in span]
    root_left = [left(x) for x in root]
    middle = [plus(1.5, -0.5 * dot_nn(root_left[a], right(current[a]))) for a in span]
    middle_right = [right(x) for x in middle]
    current = [dot_nn(left(current[a]), middle_right[a]) for a in span]
    root = [dot_nn(root_left[a], middle_right[a]) for a in span]
    root_left = [left(x) for x in root]
    middle = [plus(1.5, -0.5 * dot_nn(root_left[a], right(current[a]))) for a in span]
    root = [dot_nn(root_left[a], right(middle[a])) for a in span]
    for a in span:
        inverse = root[a] * scale[a]
        inner = jnp.sum(inverse * forcing[:, a : a + 1], axis=0, keepdims=True)
        mean_weights = jnp.sum(inverse * inner, axis=1, keepdims=True)
        transform_ref[a] = (mean_weights + jnp.sqrt(members - 1.0) * inverse).astype(bf16)
    half = second_ref.shape[0]
    segments = [
        (first_ref[0:half, :], first_mix[0:half, :]),
        (first_ref[half:, :], first_mix[half:, :]),
        (second_ref[...], second_mix[...]),
    ]
    parts = blended_parts(segments, lambda q: transform_ref[q], points)
    to_first_ref[0:half, :] = parts[0].astype(bf16)
    to_first_ref[half:, :] = parts[1].astype(bf16)
    to_second_ref[...] = parts[2].astype(bf16)


def own_kernel(transform_ref, own_ref, own_mix, column_ref, out_ref):
    points = transform_ref.shape[0]
    half = own_ref.shape[0] // 2
    segments = [
        (own_ref[0:half, :], own_mix[0:half, :]),
        (own_ref[half:, :], own_mix[half:, :]),
    ]
    parts = blended_parts(segments, lambda q: transform_ref[q], points)
    for u in range(2):
        rows = slice(u * half, (u + 1) * half)
        out_ref[rows, :] = parts[u] + column_ref[rows, 0:1]


def mixing_columns(blending, band, row, row_count, points, valid):
    slab = blending.shape[1]
    half = slab // 2
    size = slab // (4 * points)
    mixing = blending / jnp.sum(blending, axis=0, keepdims=True)
    cell = jnp.arange(slab, dtype=jnp.int32)
    step = row - jnp.clip(band - 1 + cell // half, 0, row_count - 2)
    usable = valid & (step >= 0) & (step <= 1)
    group = cell % half // size
    base = jnp.clip(group // 2 - 1 + group % 2, 0, points - 2)
    pair = jnp.where(step == 0, mixing[0:2], mixing[2:4])
    pair = jnp.where(usable, pair, 0.0)
    rows = [
        jnp.where(base == q, pair[0], jnp.where(base == q - 1, pair[1], 0.0))
        for q in range(points)
    ]
    return jnp.stack(rows, axis=0).T


def per_device(ensemble, reports, report_count, report_cell, report_weight, blending):
    local_members, cell_count = ensemble.shape
    regions = lax.axis_size("region")
    groups = lax.axis_size("member")
    members = local_members * groups
    points = report_weight.shape[1]
    slots = reports.shape[1]
    slab = cell_count // groups
    half = slab // 2
    region = lax.axis_index("region")
    member = lax.axis_index("member")
    devices = regions * groups
    region_bits = regions.bit_length() - 1
    member_bits = groups.bit_length() - 1

    def swap(x, mask):
        return lax.ppermute(x, AXES, [(i, i ^ mask) for i in range(devices)])

    def across(i):
        position = i % groups
        other = (position + 1 if position % 2 else position - 1) % groups
        return i - position + other

    def cross(x):
        return lax.ppermute(x, AXES, [(i, across(i)) for i in range(devices)])

    member_masks = [(1 << k) | 1 for k in range(member_bits - 1, 0, -1)] + [1]

    border = ensemble[:, :MARGIN][None]
    for k in range(region_bits - 1, -1, -1):
        border = jnp.concatenate([border, swap(border, (groups << k) | 1)], axis=0)

    pieces, offsets = [ensemble], [0]
    for mask in member_masks:
        pieces = pieces + [swap(x, mask) for x in pieces]
        offsets = offsets + [offset ^ mask for offset in offsets]
    partner_blending = swap(blending, 1)
    other_blending = cross(blending)

    holder = report_cell[0] // cell_count
    outside = holder != region
    first_source = jnp.min(jnp.where(outside, holder, regions))
    second_source = jnp.max(jnp.where(outside, holder, -1))
    first_source = jnp.where(first_source == regions, region, first_source)
    second_source = jnp.where(second_source < 0, region, second_source)

    def place(source):
        distance = region ^ source
        index = jnp.int32(0)
        flips = jnp.int32(0)
        for k in range(region_bits):
            bit = (distance >> k) & 1
            index = index + (bit << (region_bits - 1 - k))
            flips = flips ^ bit
        return index, flips

    first_place, first_flip = place(first_source)
    second_place, second_flip = place(second_source)
    picked = jnp.concatenate(
        [
            lax.dynamic_slice_in_dim(border, first_place, 1, axis=0),
            lax.dynamic_slice_in_dim(border, second_place, 1, axis=0),
        ],
        axis=0,
    )
    margin_pieces = [picked]
    for mask in member_masks:
        if len(margin_pieces) == 1:
            margin_pieces = margin_pieces + [swap(margin_pieces[0], mask)]
        else:
            joined = swap(jnp.concatenate(margin_pieces, axis=0), mask)
            margin_pieces = margin_pieces + [
                joined[2 * i : 2 * i + 2] for i in range(len(margin_pieces))
            ]

    table_rows = cell_count // LANES + 2
    numbers = jnp.stack(
        [region, first_source, second_source, report_count[0], jnp.int32(cell_count)]
    )
    (table,) = call(
        functools.partial(weights_kernel, table_rows),
        [((table_rows, 2 * points, LANES), f32)],
        1,
        (numbers, report_cell, report_weight, reports),
        2 * 2 * table_rows * 2 * points * slots * LANES,
        200000,
    )

    anomaly, mean = call(
        functools.partial(anomaly_kernel, tuple(offsets)),
        [((members, cell_count), bf16), ((1, cell_count), f32)],
        1,
        (member[None], *pieces),
        4 * members * cell_count,
        4 * members * cell_count,
    )
    products, forcing = call(
        products_kernel,
        [((points, members, members), f32), ((2 * points, members), f32)],
        0,
        (anomaly, mean, table),
        2 * points * members * members * cell_count,
        2 * members * cell_count + 4 * points * members * members,
    )

    odd = member % 2
    partner = member ^ 1
    other = (member - 1 + 2 * odd) % groups
    inner = (member > 0) & (member < groups - 1)
    other_half = other * slab + (1 - odd) * half
    own_mix = mixing_columns(blending, member, member, groups, points, True)
    first_mix = mixing_columns(partner_blending, partner, member, groups, points, True)
    other_mix = mixing_columns(other_blending, other, member, groups, points, inner)
    second_mix = lax.dynamic_slice_in_dim(other_mix, (1 - odd) * half, half, axis=0)
    own_cells, first_cells, second_cells, column = call(
        transpose_kernel,
        [
            ((slab, members), bf16),
            ((slab, members), bf16),
            ((half, members), bf16),
            ((slab, 8), f32),
        ],
        1,
        (jnp.stack([member * slab, partner * slab, other_half]), anomaly, mean),
        3 * slab * members,
        8 * slab * members,
    )

    transform, to_first, to_second = call(
        functools.partial(transform_kernel, tuple(offsets)),
        [
            ((points, members, members), bf16),
            ((slab, members), bf16),
            ((half, members), bf16),
        ],
        1,
        (
            jnp.stack([member, first_flip, second_flip]),
            *margin_pieces,
            table[table_rows - 2 :],
            products,
            forcing,
            first_cells,
            second_cells,
            first_mix,
            second_mix,
        ),
        2 * 26 * points * members**3,
        4 * points * members * members * 2,
        scratch=[pltpu.VMEM((members, 2 * LANES), bf16)],
    )
    from_other = cross(to_second)
    from_partner = swap(to_first, 1)
    (own,) = call(
        own_kernel,
        [((slab, members), f32)],
        0,
        (transform, own_cells, own_mix, column),
        4 * slab * members * members,
        8 * slab * members,
    )
    upper = jnp.where(odd == 0, from_other.astype(f32), 0.0)
    lower = jnp.where(odd == 1, from_other.astype(f32), 0.0)
    total = own + from_partner.astype(f32) + jnp.concatenate([upper, lower], axis=0)
    return total.astype(bf16)


def solution(mesh):
    return jax.shard_map(
        per_device,
        mesh=mesh,
        in_specs=(
            P("member", "region"),
            P("region", None),
            P("region"),
            P("region", None),
            P("region", "member", None),
            P(None, ("region", "member")),
        ),
        out_specs=P(("region", "member"), None),
        check_vma=False,
    )
```

```python
import functools

import jax
import jax.numpy as jnp
from jax import lax
from jax.experimental import pallas as pl
from jax.experimental.pallas import tpu as pltpu
from jax.sharding import PartitionSpec as P

MARGIN = 128
LANES = 128
GRANT = 20 << 20
AXES = ("region", "member")

f32 = jnp.float32
bf16 = jnp.bfloat16

VMEM = pl.BlockSpec(memory_space=pltpu.VMEM)
SMEM = pl.BlockSpec(memory_space=pltpu.SMEM)


def dot_nn(a, b):
    return lax.dot_general(a, b, (((1,), (0,)), ((), ())), preferred_element_type=f32)


def dot_nt(a, b):
    return lax.dot_general(a, b, (((1,), (1,)), ((), ())), preferred_element_type=f32)


def split(x):
    high = x.astype(bf16)
    return high, (x - high.astype(f32)).astype(bf16)


def call(kernel, outs, inputs, flops, moved, smem_in=0, smem_out=0, scratch=()):
    return pl.pallas_call(
        kernel,
        out_shape=[jax.ShapeDtypeStruct(s, d) for s, d in outs],
        in_specs=[SMEM] * smem_in + [VMEM] * (len(inputs) - smem_in),
        out_specs=[VMEM] * (len(outs) - smem_out) + [SMEM] * smem_out,
        scratch_shapes=list(scratch),
        cost_estimate=pl.CostEstimate(flops=flops, bytes_accessed=moved, transcendentals=0),
        compiler_params=pltpu.CompilerParams(vmem_limit_bytes=GRANT),
    )(*inputs)


def parts_of(x, size):
    if size & (size - 1):
        return lax.div(x, size), lax.rem(x, size)
    return lax.shift_right_logical(x, size.bit_length() - 1), x & (size - 1)


def weights_kernel(cells, regions, live_ref, cell_ref, weight_ref, report_ref, table_ref, source_ref):
    region = lax.axis_index("region")
    bits = regions.bit_length() - 1
    points, slots = weight_ref.shape[1:]
    rows = cells // LANES + 2
    holder, within = parts_of(cell_ref[...], cells)
    block, low = parts_of(within, LANES)
    outside = holder != region
    named = holder.astype(f32)
    first = jnp.min(jnp.where(outside, named, float(regions))).astype(jnp.int32)
    second = jnp.max(jnp.where(outside, named, -1.0)).astype(jnp.int32)
    first = jnp.where(first == regions, region, first)
    second = jnp.where(second < 0, region, second)
    for j, source in enumerate((first, second)):
        distance = region ^ source
        place = jnp.int32(0)
        flip = jnp.int32(0)
        for k in range(bits):
            bit = (distance >> k) & 1
            place = place + (bit << (bits - 1 - k))
            flip = flip ^ bit
        source_ref[j] = place
        source_ref[2 + j] = flip
    high = jnp.where(outside, jnp.where(holder == first, rows - 2, rows - 1), block)
    active = lax.broadcasted_iota(jnp.int32, (1, slots), 1) < live_ref[0]
    weights = jnp.where(active, weight_ref[0], 0.0)
    values = jnp.concatenate([weights, weights * report_ref[...]], axis=0)
    low_hot = (lax.broadcasted_iota(jnp.int32, (LANES, slots), 0) == low).astype(f32).astype(bf16)
    chosen = jnp.concatenate(
        [jnp.where(high == row, values, 0.0) for row in range(rows)], axis=0
    )
    first, second = split(chosen)
    total = dot_nt(first, low_hot) + dot_nt(second, low_hot)
    table_ref[...] = total.reshape(rows, 2 * points, LANES)


def pick_kernel(source_ref, near_ref, far_ref, out_ref):
    count = near_ref.shape[0]
    for j in range(2):
        place = source_ref[j]
        inside = jnp.minimum(place, count - 1)
        outside = jnp.maximum(place - count, 0)
        out_ref[j] = jnp.where(place < count, near_ref[inside], far_ref[outside])


def anomaly_kernel(offsets, *refs):
    pieces, (anomaly_ref, mean_ref) = refs[:-2], refs[-2:]
    member = lax.axis_index("member")
    rows = pieces[0].shape[0]
    members = rows * len(pieces)
    total = jnp.sum(pieces[0][...].astype(f32), axis=0, keepdims=True)
    for piece in pieces[1:]:
        total = total + jnp.sum(piece[...].astype(f32), axis=0, keepdims=True)
    mean = total / members
    mean_ref[...] = mean
    for offset, piece in zip(offsets, pieces):
        start = pl.multiple_of((member ^ offset) * rows, rows)
        anomaly_ref[pl.ds(start, rows), :] = (piece[...].astype(f32) - mean).astype(bf16)


def products_kernel(anomaly_ref, mean_ref, table_ref, products_ref, forcing_ref):
    members, cells = anomaly_ref.shape
    points = products_ref.shape[0]
    chunk = min(cells, 2048)
    forcing = None
    for start in range(0, cells, chunk):
        block = anomaly_ref[:, start : start + chunk]
        departures = []
        for a in range(points):
            scaled = []
            for h in range(start // LANES, (start + chunk) // LANES):
                lanes = slice(h * LANES, (h + 1) * LANES)
                scaled.append(
                    (anomaly_ref[:, lanes].astype(f32) * table_ref[h, a : a + 1, :]).astype(bf16)
                )
            part = dot_nt(jnp.concatenate(scaled, axis=1), block)
            if start == 0:
                products_ref[a] = part
            else:
                products_ref[a] += part
        for h in range(start // LANES, (start + chunk) // LANES):
            lanes = slice(h * LANES, (h + 1) * LANES)
            tile = table_ref[h]
            departures.append(tile[points:, :] - tile[:points, :] * mean_ref[:, lanes])
        departure = jnp.concatenate(departures, axis=1)
        first, second = split(jnp.concatenate([departure, departure], axis=0))
        part = dot_nt(first, block) + dot_nt(second, block)
        forcing = part if forcing is None else forcing + part
    forcing_ref[...] = forcing


def cells_kernel(
    row_count, points, anomaly_ref, mean_ref, own_blend, first_blend, second_blend,
    own_ref, first_ref, second_ref, own_mix, first_mix, second_mix, column_ref
):
    member = lax.axis_index("member")
    odd = member & 1
    partner = member ^ 1
    other = member - 1 + 2 * odd
    exists = (other >= 0) & (other < row_count)
    other = jnp.where(exists, other, 0)
    slab = own_ref.shape[0]
    half = slab // 2
    for ref, band in ((own_ref, member), (first_ref, partner)):
        for u in range(2):
            start = pl.multiple_of(band * slab + u * half, half)
            ref[u * half : (u + 1) * half, :] = anomaly_ref[:, pl.ds(start, half)].T
    start = pl.multiple_of(other * slab + (1 - odd) * half, half)
    second_ref[...] = anomaly_ref[:, pl.ds(start, half)].T
    row = mean_ref[:, pl.ds(pl.multiple_of(member * slab, slab), slab)]
    column_ref[...] = jnp.broadcast_to(row, (8, slab)).T
    cell = lax.broadcasted_iota(jnp.int32, (1, slab), 1)
    upper = cell < half
    bases = column_bases(points)
    size = half // len(bases)
    inside = jnp.where(upper, cell, cell - half)
    base = jnp.zeros_like(cell)
    for g in range(1, len(bases)):
        base = base + jnp.where(inside >= g * size, bases[g] - bases[g - 1], 0)

    def columns(blend_ref, band, valid):
        blending = blend_ref[...]
        mixing = blending / jnp.sum(blending, axis=0, keepdims=True)
        tops = [jnp.clip(band - 1 + u, 0, row_count - 2) for u in range(2)]
        step = member - jnp.where(upper, tops[0], tops[1])
        pairs = []
        for c in range(2):
            pair = jnp.where(
                step == 0, mixing[c : c + 1], jnp.where(step == 1, mixing[2 + c : 3 + c], 0.0)
            )
            pairs.append(jnp.where(valid, pair, 0.0))
        rows = [
            jnp.where(base == q, pairs[0], jnp.where(base == q - 1, pairs[1], 0.0))
            for q in range(points)
        ]
        rows = rows + [jnp.zeros_like(rows[0])] * (-points % 8)
        return jnp.concatenate(rows, axis=0)

    own_mix[...] = columns(own_blend, member, True).T
    first_mix[...] = columns(first_blend, partner, True).T
    second = columns(second_blend, other, exists)
    second = jnp.where(odd == 1, second[:, :half], second[:, half:])
    second_mix[...] = second.T


def column_bases(points):
    return [min(max(b - 1 + v, 0), points - 2) for b in range(points) for v in range(2)]


def blended_parts(segments, transforms, points):
    half = segments[0][0].shape[0]
    bases = column_bases(points)
    size = half // len(bases)
    spans = []
    for v in range(points - 1):
        hits = [g for g, b in enumerate(bases) if b == v]
        spans.append((hits[0] * size, (hits[-1] + 1) * size))
    sums = [[None] * (points - 1) for _ in segments]
    for q in range(points):
        where = [v for v in (q - 1, q) if 0 <= v <= points - 2]
        rows = [
            (n, v, cells[spans[v][0] : spans[v][1], :])
            for n, (cells, _) in enumerate(segments)
            for v in where
        ]
        spread = dot_nn(jnp.concatenate([r[2] for r in rows], axis=0), transforms(q))
        at = 0
        for n, v, cells in rows:
            low, high = spans[v]
            term = segments[n][1][low:high, q : q + 1] * spread[at : at + high - low]
            sums[n][v] = term if sums[n][v] is None else sums[n][v] + term
            at += high - low
    return [jnp.concatenate(parts, axis=0) for parts in sums]


def transform_kernel(offsets, source_ref, *refs):
    count = len(offsets)
    pieces = refs[:count]
    (
        table_ref,
        products_ref,
        forcing_ref,
        first_ref,
        second_ref,
        first_mix,
        second_mix,
        transform_ref,
        to_first_ref,
        to_second_ref,
        margin_ref,
    ) = refs[count:]
    member = lax.axis_index("member")
    rows = pieces[0].shape[1]
    members = rows * count
    points = products_ref.shape[0]
    last = table_ref.shape[0]
    for offset, piece in zip(offsets, pieces):
        for j in range(2):
            start = pl.multiple_of((member ^ offset ^ source_ref[2 + j]) * rows, rows)
            margin_ref[pl.ds(start, rows), j * LANES : (j + 1) * LANES] = piece[j]
    values = margin_ref[...].astype(f32)
    mean = jnp.sum(values, axis=0, keepdims=True) / members
    pert = (values - mean).astype(bf16)
    pert_wide = pert.astype(f32)
    tiles = jnp.concatenate([table_ref[last - 2], table_ref[last - 1]], axis=1)
    departure = tiles[points:, :] - tiles[:points, :] * mean
    first, second = split(jnp.concatenate([departure, departure], axis=0))
    forcing = forcing_ref[...] + dot_nt(first, pert) + dot_nt(second, pert)
    forcing = forcing.T
    identity = lax.broadcasted_iota(jnp.int32, (members, members), 0) == lax.broadcasted_iota(
        jnp.int32, (members, members), 1
    )

    def plus(scalar, matrix):
        return matrix + jnp.where(identity, scalar, 0.0)

    def left(x):
        high, low = split(x)
        return jnp.concatenate([high, high, low], axis=1)

    def right(x):
        high, low = split(x)
        return jnp.concatenate([high, low, high], axis=0)

    span = range(points)
    matrix, scale = [], []
    for a in span:
        weighted = (pert_wide * tiles[a : a + 1, :]).astype(bf16)
        full = plus(members - 1.0, products_ref[a] + dot_nt(weighted, pert))
        square = jnp.sum(jnp.sum(full * full, axis=0, keepdims=True), axis=1, keepdims=True)
        frobenius = jnp.sqrt(square)
        matrix.append(full / frobenius)
        scale.append(1.0 / jnp.sqrt(frobenius))
    matrix_left = [left(x) for x in matrix]
    squared = [dot_nn(matrix_left[a], right(matrix[a])) for a in span]
    root = [
        plus(2.25, -2.4375 * matrix[a])
        + dot_nn(
            left(squared[a]),
            right(plus(1.6875, 0.0625 * squared[a] - 0.5625 * matrix[a])),
        )
        for a in span
    ]
    current = [dot_nn(matrix_left[a], right(root[a])) for a in span]
    root_left = [left(x) for x in root]
    middle = [plus(1.5, -0.5 * dot_nn(root_left[a], right(current[a]))) for a in span]
    middle_right = [right(x) for x in middle]
    current = [dot_nn(left(current[a]), middle_right[a]) for a in span]
    root = [dot_nn(root_left[a], middle_right[a]) for a in span]
    root_left = [left(x) for x in root]
    middle = [plus(1.5, -0.5 * dot_nn(root_left[a], right(current[a]))) for a in span]
    root = [dot_nn(root_left[a], right(middle[a])) for a in span]
    for a in span:
        inverse = root[a] * scale[a]
        inner = jnp.sum(inverse * forcing[:, a : a + 1], axis=0, keepdims=True)
        mean_weights = jnp.sum(inverse * inner, axis=1, keepdims=True)
        transform_ref[a] = (mean_weights + jnp.sqrt(members - 1.0) * inverse).astype(bf16)
    half = second_ref.shape[0]
    segments = [
        (first_ref[0:half, :], first_mix[0:half, :]),
        (first_ref[half:, :], first_mix[half:, :]),
        (second_ref[...], second_mix[...]),
    ]
    parts = blended_parts(segments, lambda q: transform_ref[q], points)
    to_first_ref[0:half, :] = parts[0].astype(bf16)
    to_first_ref[half:, :] = parts[1].astype(bf16)
    to_second_ref[...] = parts[2].astype(bf16)


def own_kernel(transform_ref, own_ref, own_mix, column_ref, out_ref):
    points = transform_ref.shape[0]
    half = own_ref.shape[0] // 2
    segments = [
        (own_ref[0:half, :], own_mix[0:half, :]),
        (own_ref[half:, :], own_mix[half:, :]),
    ]
    parts = blended_parts(segments, lambda q: transform_ref[q], points)
    for u in range(2):
        rows = slice(u * half, (u + 1) * half)
        out_ref[rows, :] = parts[u] + column_ref[rows, 0:1]


def per_device(ensemble, reports, report_count, report_cell, report_weight, blending):
    local_members, cell_count = ensemble.shape
    regions = lax.axis_size("region")
    groups = lax.axis_size("member")
    members = local_members * groups
    points = report_weight.shape[1]
    slots = reports.shape[1]
    slab = cell_count // groups
    half = slab // 2
    devices = regions * groups
    region_bits = regions.bit_length() - 1
    member_bits = groups.bit_length() - 1

    def swap(name, x, mask):
        with jax.named_scope(name):
            return lax.ppermute(x, AXES, [(i, i ^ mask) for i in range(devices)])

    def across(i):
        position = i % groups
        other = (position + 1 if position % 2 else position - 1) % groups
        return i - position + other

    def cross(name, x):
        with jax.named_scope(name):
            return lax.ppermute(x, AXES, [(i, across(i)) for i in range(devices)])

    member_masks = [(1 << k) | 1 for k in range(member_bits - 1, 0, -1)] + [1]

    table_rows = cell_count // LANES + 2
    with jax.named_scope("kernel_weights"):
        table, sources = call(
            functools.partial(weights_kernel, cell_count, regions),
            [((table_rows, 2 * points, LANES), f32), ((4,), jnp.int32)],
            (report_count, report_cell, report_weight, reports),
            4 * table_rows * 2 * points * slots * LANES,
            100000,
            smem_in=1,
            smem_out=1,
        )

    near = ensemble[:, :MARGIN][None]
    for step, k in enumerate(range(region_bits - 1, -1, -1)):
        far = swap(f"margin_{step}", near, (groups << k) | 1)
        if k:
            near = jnp.concatenate([near, far], axis=0)
    with jax.named_scope("kernel_pick"):
        (picked,) = call(
            pick_kernel,
            [((2, local_members, MARGIN), bf16)],
            (sources, near, far),
            0,
            100000,
            smem_in=1,
        )
    margins = [picked]
    for step, mask in enumerate(member_masks):
        if step == 0:
            margins = margins + [swap("spread_0", picked, mask)]
        else:
            joined = swap(f"spread_{step}", jnp.concatenate(margins, axis=0), mask)
            margins = margins + [joined[2 * i : 2 * i + 2] for i in range(len(margins))]

    pieces, offsets = [ensemble], [0]
    for step, mask in enumerate(member_masks):
        pieces = pieces + [swap(f"whole_{step}_{i}", x, mask) for i, x in enumerate(pieces)]
        offsets = offsets + [offset ^ mask for offset in offsets]
    partner_blending = swap("blend_partner", blending, 1)
    other_blending = cross("blend_other", blending)

    with jax.named_scope("kernel_anomaly"):
        anomaly, mean = call(
            functools.partial(anomaly_kernel, tuple(offsets)),
            [((members, cell_count), bf16), ((1, cell_count), f32)],
            tuple(pieces),
            4 * members * cell_count,
            4 * members * cell_count,
        )
    with jax.named_scope("kernel_products"):
        products, forcing = call(
            products_kernel,
            [((points, members, members), f32), ((2 * points, members), f32)],
            (anomaly, mean, table),
            2 * points * members * members * cell_count,
            2 * members * cell_count + 4 * points * members * members,
        )
    padded = points + -points % 8
    with jax.named_scope("kernel_cells"):
        own_cells, first_cells, second_cells, own_mix, first_mix, second_mix, column = call(
            functools.partial(cells_kernel, groups, points),
            [
                ((slab, members), bf16),
                ((slab, members), bf16),
                ((half, members), bf16),
                ((slab, padded), f32),
                ((slab, padded), f32),
                ((half, padded), f32),
                ((slab, 8), f32),
            ],
            (anomaly, mean, blending, partner_blending, other_blending),
            3 * slab * members,
            8 * slab * members,
        )
    with jax.named_scope("kernel_transform"):
        transform, to_first, to_second = call(
            functools.partial(transform_kernel, tuple(offsets)),
            [
                ((points, members, members), bf16),
                ((slab, members), bf16),
                ((half, members), bf16),
            ],
            (
                sources,
                *margins,
                table,
                products,
                forcing,
                first_cells,
                second_cells,
                first_mix,
                second_mix,
            ),
            2 * 26 * points * members**3,
            8 * points * members * members,
            smem_in=1,
            scratch=[pltpu.VMEM((members, 2 * LANES), bf16)],
        )
    from_other = cross("back_other", to_second)
    from_partner = swap("back_partner", to_first, 1)
    with jax.named_scope("kernel_own"):
        (own,) = call(
            own_kernel,
            [((slab, members), f32)],
            (transform, own_cells, own_mix, column),
            4 * slab * members * members,
            8 * slab * members,
        )
    odd = lax.axis_index("member") % 2
    upper = jnp.where(odd == 0, from_other.astype(f32), 0.0)
    lower = jnp.where(odd == 1, from_other.astype(f32), 0.0)
    total = own + from_partner.astype(f32) + jnp.concatenate([upper, lower], axis=0)
    return total.astype(bf16)


def solution(mesh):
    return jax.shard_map(
        per_device,
        mesh=mesh,
        in_specs=(
            P("member", "region"),
            P("region", None),
            P("region"),
            P("region", None),
            P("region", "member", None),
            P(None, ("region", "member")),
        ),
        out_specs=P(("region", "member"), None),
        check_vma=False,
    )
```

```python
import functools

import jax
import jax.numpy as jnp
from jax import lax
from jax.experimental import pallas as pl
from jax.experimental.pallas import tpu as pltpu
from jax.sharding import PartitionSpec as P


MARGIN = 128
LANES = 128
GRANT = 20 << 20
AXES = ("region", "member")

f32 = jnp.float32
bf16 = jnp.bfloat16

VMEM = pl.BlockSpec(memory_space=pltpu.VMEM)
SMEM = pl.BlockSpec(memory_space=pltpu.SMEM)


def dot_nn(a, b):
    return lax.dot_general(a, b, (((1,), (0,)), ((), ())), preferred_element_type=f32)


def dot_nt(a, b):
    return lax.dot_general(a, b, (((1,), (1,)), ((), ())), preferred_element_type=f32)


def split(x):
    high = x.astype(bf16)
    return high, (x - high.astype(f32)).astype(bf16)


def call(kernel, outs, inputs, flops, moved, smem_in=0, smem_out=0, scratch=()):
    return pl.pallas_call(
        kernel,
        out_shape=[jax.ShapeDtypeStruct(s, d) for s, d in outs],
        in_specs=[SMEM] * smem_in + [VMEM] * (len(inputs) - smem_in),
        out_specs=[VMEM] * (len(outs) - smem_out) + [SMEM] * smem_out,
        scratch_shapes=list(scratch),
        cost_estimate=pl.CostEstimate(flops=flops, bytes_accessed=moved, transcendentals=0),
        compiler_params=pltpu.CompilerParams(vmem_limit_bytes=GRANT),
    )(*inputs)


def parts_of(x, size):
    if size & (size - 1):
        return lax.div(x, size), lax.rem(x, size)
    return lax.shift_right_logical(x, size.bit_length() - 1), x & (size - 1)


def weights_kernel(cells, regions, live_ref, cell_ref, weight_ref, report_ref, table_ref, place_ref, flip_ref):
    region = lax.axis_index("region")
    bits = regions.bit_length() - 1
    points, slots = weight_ref.shape[1:]
    rows = cells // LANES + 2
    holder, within = parts_of(cell_ref[...], cells)
    block, low = parts_of(within, LANES)
    outside = holder != region
    named = holder.astype(f32)
    first = jnp.min(jnp.where(outside, named, float(regions))).astype(jnp.int32)
    second = jnp.max(jnp.where(outside, named, -1.0)).astype(jnp.int32)
    first = jnp.where(first == regions, region, first)
    second = jnp.where(second < 0, region, second)
    for j, source in enumerate((first, second)):
        distance = region ^ source
        place = jnp.int32(0)
        flip = jnp.int32(0)
        for k in range(bits):
            bit = (distance >> k) & 1
            place = place + (bit << (bits - 1 - k))
            flip = flip ^ bit
        place_ref[j : j + 1, :] = jnp.full((1, LANES), place, jnp.int32)
        flip_ref[j] = flip
    high = jnp.where(outside, jnp.where(holder == first, rows - 2, rows - 1), block)
    active = lax.broadcasted_iota(jnp.int32, (1, slots), 1) < live_ref[0]
    weights = jnp.where(active, weight_ref[0], 0.0)
    values = jnp.concatenate([weights, weights * report_ref[...]], axis=0)
    low_hot = (lax.broadcasted_iota(jnp.int32, (LANES, slots), 0) == low).astype(f32).astype(bf16)
    chosen = jnp.concatenate(
        [jnp.where(high == row, values, 0.0) for row in range(rows)], axis=0
    )
    first, second = split(chosen)
    total = dot_nt(first, low_hot) + dot_nt(second, low_hot)
    table_ref[...] = total.reshape(rows, 2 * points, LANES)


def pick_kernel(place_ref, near_ref, far_ref, out_ref):
    count = near_ref.shape[0]
    for j in range(2):
        place = jnp.broadcast_to(place_ref[j : j + 1, :], near_ref.shape[1:])
        chosen = jnp.zeros(near_ref.shape[1:], f32)
        for ref, base in ((near_ref, 0), (far_ref, count)):
            for i in range(count):
                chosen = jnp.where(place == base + i, ref[i].astype(f32), chosen)
        out_ref[j] = chosen.astype(bf16)


def anomaly_kernel(offsets, *refs):
    pieces, (anomaly_ref, mean_ref) = refs[:-2], refs[-2:]
    member = lax.axis_index("member")
    rows = pieces[0].shape[0]
    members = rows * len(pieces)
    total = jnp.sum(pieces[0][...].astype(f32), axis=0, keepdims=True)
    for piece in pieces[1:]:
        total = total + jnp.sum(piece[...].astype(f32), axis=0, keepdims=True)
    mean = total / members
    mean_ref[...] = mean
    for offset, piece in zip(offsets, pieces):
        start = pl.multiple_of((member ^ offset) * rows, rows)
        anomaly_ref[pl.ds(start, rows), :] = (piece[...].astype(f32) - mean).astype(bf16)


def products_kernel(anomaly_ref, mean_ref, table_ref, products_ref, forcing_ref):
    _, cells = anomaly_ref.shape
    points = products_ref.shape[0]
    chunk = min(cells, 2048)
    forcing = None
    for start in range(0, cells, chunk):
        block = anomaly_ref[:, start : start + chunk]
        departures = []
        for a in range(points):
            scaled = []
            for h in range(start // LANES, (start + chunk) // LANES):
                lanes = slice(h * LANES, (h + 1) * LANES)
                scaled.append(
                    (anomaly_ref[:, lanes].astype(f32) * table_ref[h, a : a + 1, :]).astype(bf16)
                )
            part = dot_nt(jnp.concatenate(scaled, axis=1), block)
            if start == 0:
                products_ref[a] = part
            else:
                products_ref[a] += part
        for h in range(start // LANES, (start + chunk) // LANES):
            lanes = slice(h * LANES, (h + 1) * LANES)
            tile = table_ref[h]
            departures.append(tile[points:, :] - tile[:points, :] * mean_ref[:, lanes])
        departure = jnp.concatenate(departures, axis=1)
        first, second = split(jnp.concatenate([departure, departure], axis=0))
        part = dot_nt(first, block) + dot_nt(second, block)
        forcing = part if forcing is None else forcing + part
    forcing_ref[...] = forcing


def cells_kernel(
    row_count, points, anomaly_ref, mean_ref, own_blend, first_blend, second_blend,
    own_ref, first_ref, second_ref, own_mix, first_mix, second_mix, column_ref
):
    member = lax.axis_index("member")
    odd = member & 1
    partner = member ^ 1
    other = member - 1 + 2 * odd
    exists = (other >= 0) & (other < row_count)
    other = jnp.where(exists, other, 0)
    slab = own_ref.shape[0]
    half = slab // 2
    for ref, band in ((own_ref, member), (first_ref, partner)):
        for u in range(2):
            start = pl.multiple_of(band * slab + u * half, half)
            ref[u * half : (u + 1) * half, :] = anomaly_ref[:, pl.ds(start, half)].T
    start = pl.multiple_of(other * slab + (1 - odd) * half, half)
    second_ref[...] = anomaly_ref[:, pl.ds(start, half)].T
    row = mean_ref[:, pl.ds(pl.multiple_of(member * slab, slab), slab)]
    column_ref[...] = jnp.broadcast_to(row, (8, slab)).T
    cell = lax.broadcasted_iota(jnp.int32, (1, slab), 1)
    upper = cell < half
    bases = column_bases(points)
    size = half // len(bases)
    inside = jnp.where(upper, cell, cell - half)
    base = jnp.zeros_like(cell)
    for g in range(1, len(bases)):
        base = base + jnp.where(inside >= g * size, bases[g] - bases[g - 1], 0)

    def columns(blend_ref, band, valid):
        blending = blend_ref[...]
        mixing = blending / jnp.sum(blending, axis=0, keepdims=True)
        tops = [jnp.clip(band - 1 + u, 0, row_count - 2) for u in range(2)]
        step = member - jnp.where(upper, tops[0], tops[1])
        pairs = []
        for c in range(2):
            pair = jnp.where(
                step == 0, mixing[c : c + 1], jnp.where(step == 1, mixing[2 + c : 3 + c], 0.0)
            )
            pairs.append(jnp.where(valid, pair, 0.0))
        rows = [
            jnp.where(base == q, pairs[0], jnp.where(base == q - 1, pairs[1], 0.0))
            for q in range(points)
        ]
        rows = rows + [jnp.zeros_like(rows[0])] * (-points % 8)
        return jnp.concatenate(rows, axis=0)

    own_mix[...] = columns(own_blend, member, True).T
    first_mix[...] = columns(first_blend, partner, True).T
    second = columns(second_blend, other, exists)
    second = jnp.where(odd == 1, second[:, :half], second[:, half:])
    second_mix[...] = second.T


def column_bases(points):
    return [min(max(b - 1 + v, 0), points - 2) for b in range(points) for v in range(2)]


def blended_parts(segments, transforms, points):
    half = segments[0][0].shape[0]
    bases = column_bases(points)
    size = half // len(bases)
    spans = []
    for v in range(points - 1):
        hits = [g for g, b in enumerate(bases) if b == v]
        spans.append((hits[0] * size, (hits[-1] + 1) * size))
    sums = [[None] * (points - 1) for _ in segments]
    for q in range(points):
        where = [v for v in (q - 1, q) if 0 <= v <= points - 2]
        rows = [
            (n, v, cells[spans[v][0] : spans[v][1], :])
            for n, (cells, _) in enumerate(segments)
            for v in where
        ]
        spread = dot_nn(jnp.concatenate([r[2] for r in rows], axis=0), transforms(q))
        at = 0
        for n, v, cells in rows:
            low, high = spans[v]
            term = segments[n][1][low:high, q : q + 1] * spread[at : at + high - low]
            sums[n][v] = term if sums[n][v] is None else sums[n][v] + term
            at += high - low
    return [jnp.concatenate(parts, axis=0) for parts in sums]


def transform_kernel(offsets, flip_ref, *refs):
    count = len(offsets)
    pieces = refs[:count]
    (
        table_ref,
        products_ref,
        forcing_ref,
        first_ref,
        second_ref,
        first_mix,
        second_mix,
        transform_ref,
        to_first_ref,
        to_second_ref,
        margin_ref,
    ) = refs[count:]
    member = lax.axis_index("member")
    rows = pieces[0].shape[1]
    members = rows * count
    points = products_ref.shape[0]
    last = table_ref.shape[0]
    for offset, piece in zip(offsets, pieces):
        for j in range(2):
            start = pl.multiple_of((member ^ offset ^ flip_ref[j]) * rows, rows)
            margin_ref[pl.ds(start, rows), j * LANES : (j + 1) * LANES] = piece[j]
    values = margin_ref[...].astype(f32)
    mean = jnp.sum(values, axis=0, keepdims=True) / members
    pert = (values - mean).astype(bf16)
    pert_wide = pert.astype(f32)
    tiles = jnp.concatenate([table_ref[last - 2], table_ref[last - 1]], axis=1)
    departure = tiles[points:, :] - tiles[:points, :] * mean
    first, second = split(jnp.concatenate([departure, departure], axis=0))
    forcing = forcing_ref[...] + dot_nt(first, pert) + dot_nt(second, pert)
    forcing = forcing.T
    identity = lax.broadcasted_iota(jnp.int32, (members, members), 0) == lax.broadcasted_iota(
        jnp.int32, (members, members), 1
    )

    def plus(scalar, matrix):
        return matrix + jnp.where(identity, scalar, 0.0)

    span = range(points)
    matrix, scale = [], []
    for a in span:
        weighted = (pert_wide * tiles[a : a + 1, :]).astype(bf16)
        full = plus(members - 1.0, products_ref[a] + dot_nt(weighted, pert))
        square = jnp.sum(jnp.sum(full * full, axis=0, keepdims=True), axis=1, keepdims=True)
        frobenius = jnp.sqrt(square)
        matrix.append(full / frobenius)
        scale.append(1.0 / jnp.sqrt(frobenius))
    low = [x.astype(bf16) for x in matrix]
    squared = [dot_nn(x, x) for x in low]
    root = [
        1.6875 * squared[a]
        - 2.4375 * matrix[a]
        + dot_nn(
            squared[a].astype(bf16), (0.0625 * squared[a] - 0.5625 * matrix[a]).astype(bf16)
        )
        for a in span
    ]
    root_low = [x.astype(bf16) for x in root]
    current = [2.25 * matrix[a] + dot_nn(low[a], root_low[a]) for a in span]
    current_low = [x.astype(bf16) for x in current]
    middle = [
        plus(0.125, -1.125 * current[a] - 0.5 * dot_nn(root_low[a], current_low[a])) for a in span
    ]
    middle_low = [x.astype(bf16) for x in middle]
    root = [
        plus(0.34375, 1.375 * root[a] + 2.25 * middle[a] + dot_nn(root_low[a], middle_low[a]))
        for a in span
    ]
    current = [1.375 * current[a] + dot_nn(current_low[a], middle_low[a]) for a in span]
    root_low = [x.astype(bf16) for x in root]
    middle = [
        plus(0.25, -1.375 * current[a] - 0.5 * dot_nn(root_low[a], current[a].astype(bf16)))
        for a in span
    ]
    root = [
        plus(3.4375, 1.25 * root[a] + 2.75 * middle[a])
        + dot_nn(root_low[a], middle[a].astype(bf16))
        for a in span
    ]
    for a in span:
        inverse = root[a] * scale[a]
        inner = jnp.sum(inverse * forcing[:, a : a + 1], axis=0, keepdims=True)
        mean_weights = jnp.sum(inverse * inner, axis=1, keepdims=True)
        transform_ref[a] = (mean_weights + jnp.sqrt(members - 1.0) * inverse).astype(bf16)
    half = second_ref.shape[0]
    segments = [
        (first_ref[0:half, :], first_mix[0:half, :]),
        (first_ref[half:, :], first_mix[half:, :]),
        (second_ref[...], second_mix[...]),
    ]
    parts = blended_parts(segments, lambda q: transform_ref[q], points)
    to_first_ref[0:half, :] = parts[0].astype(bf16)
    to_first_ref[half:, :] = parts[1].astype(bf16)
    to_second_ref[...] = parts[2].astype(bf16)


def own_kernel(transform_ref, own_ref, own_mix, column_ref, out_ref):
    points = transform_ref.shape[0]
    half = own_ref.shape[0] // 2
    segments = [
        (own_ref[0:half, :], own_mix[0:half, :]),
        (own_ref[half:, :], own_mix[half:, :]),
    ]
    parts = blended_parts(segments, lambda q: transform_ref[q], points)
    for u in range(2):
        rows = slice(u * half, (u + 1) * half)
        out_ref[rows, :] = parts[u] + column_ref[rows, 0:1]


def per_device(ensemble, reports, report_count, report_cell, report_weight, blending):
    local_members, cell_count = ensemble.shape
    regions = lax.axis_size("region")
    groups = lax.axis_size("member")
    members = local_members * groups
    points = report_weight.shape[1]
    slots = reports.shape[1]
    slab = cell_count // groups
    half = slab // 2
    devices = regions * groups
    region_bits = regions.bit_length() - 1
    member_bits = groups.bit_length() - 1

    def swap(x, mask):
        return lax.ppermute(x, AXES, [(i, i ^ mask) for i in range(devices)])

    def across(i):
        position = i % groups
        if position in (0, groups - 1):
            return (i + groups * (1 - 2 * (i // groups % 2))) if regions > 1 else i
        return i + (1 if position % 2 else -1)

    def cross(x):
        return lax.ppermute(x, AXES, [(i, across(i)) for i in range(devices)])

    member_masks = [(1 << k) | 1 for k in range(member_bits - 1, 0, -1)] + [1]

    table_rows = cell_count // LANES + 2
    table, places, flips = call(
        functools.partial(weights_kernel, cell_count, regions),
        [
            ((table_rows, 2 * points, LANES), f32),
            ((2, LANES), jnp.int32),
            ((2,), jnp.int32),
        ],
        (report_count, report_cell, report_weight, reports),
        4 * table_rows * 2 * points * slots * LANES,
        100000,
        smem_in=1,
        smem_out=1,
    )

    near = ensemble[:, :MARGIN][None]
    for k in range(region_bits - 1, -1, -1):
        far = swap(near, (groups << k) | 1)
        if k:
            near = jnp.concatenate([near, far], axis=0)
    (picked,) = call(
        pick_kernel,
        [((2, local_members, MARGIN), bf16)],
        (places, near, far),
        0,
        100000,
    )
    margins = [picked]
    for step, mask in enumerate(member_masks):
        if step == 0:
            margins = margins + [swap(picked, mask)]
        else:
            joined = swap(jnp.concatenate(margins, axis=0), mask)
            margins = margins + [joined[2 * i : 2 * i + 2] for i in range(len(margins))]

    pieces, offsets = [ensemble], [0]
    for mask in member_masks:
        pieces = pieces + [swap(x, mask) for x in pieces]
        offsets = offsets + [offset ^ mask for offset in offsets]
    partner_blending = swap(blending, 1)
    other_blending = cross(blending)

    anomaly, mean = call(
        functools.partial(anomaly_kernel, tuple(offsets)),
        [((members, cell_count), bf16), ((1, cell_count), f32)],
        tuple(pieces),
        4 * members * cell_count,
        4 * members * cell_count,
    )
    products, forcing = call(
        products_kernel,
        [((points, members, members), f32), ((2 * points, members), f32)],
        (anomaly, mean, table),
        2 * points * members * members * cell_count,
        2 * members * cell_count + 4 * points * members * members,
    )
    padded = points + -points % 8
    own_cells, first_cells, second_cells, own_mix, first_mix, second_mix, column = call(
        functools.partial(cells_kernel, groups, points),
        [
            ((slab, members), bf16),
            ((slab, members), bf16),
            ((half, members), bf16),
            ((slab, padded), f32),
            ((slab, padded), f32),
            ((half, padded), f32),
            ((slab, 8), f32),
        ],
        (anomaly, mean, blending, partner_blending, other_blending),
        3 * slab * members,
        8 * slab * members,
    )
    transform, to_first, to_second = call(
        functools.partial(transform_kernel, tuple(offsets)),
        [
            ((points, members, members), bf16),
            ((slab, members), bf16),
            ((half, members), bf16),
        ],
        (
            flips,
            *margins,
            table,
            products,
            forcing,
            first_cells,
            second_cells,
            first_mix,
            second_mix,
        ),
        2 * 26 * points * members**3,
        8 * points * members * members,
        smem_in=1,
        scratch=[pltpu.VMEM((members, 2 * LANES), bf16)],
    )
    from_other = cross(to_second)
    from_partner = swap(to_first, 1)
    (own,) = call(
        own_kernel,
        [((slab, members), f32)],
        (transform, own_cells, own_mix, column),
        4 * slab * members * members,
        8 * slab * members,
    )
    odd = lax.axis_index("member") % 2
    upper = jnp.where(odd == 0, from_other.astype(f32), 0.0)
    lower = jnp.where(odd == 1, from_other.astype(f32), 0.0)
    total = own + from_partner.astype(f32) + jnp.concatenate([upper, lower], axis=0)
    return total.astype(bf16)


def solution(mesh):
    return jax.shard_map(
        per_device,
        mesh=mesh,
        in_specs=(
            P("member", "region"),
            P("region", None),
            P("region"),
            P("region", None),
            P("region", "member", None),
            P(None, ("region", "member")),
        ),
        out_specs=P(("region", "member"), None),
        check_vma=False,
    )
```

```python
import functools

import jax
import jax.numpy as jnp
from jax import lax
from jax.experimental import pallas as pl
from jax.experimental.pallas import tpu as pltpu
from jax.sharding import PartitionSpec as P


MARGIN = 128
LANES = 128
GRANT = 20 << 20
GANG = 2
LAG = 1
AXES = ("region", "member")

f32 = jnp.float32
bf16 = jnp.bfloat16

VMEM = pl.BlockSpec(memory_space=pltpu.VMEM)
SMEM = pl.BlockSpec(memory_space=pltpu.SMEM)


def dot_nn(a, b):
    return lax.dot_general(a, b, (((1,), (0,)), ((), ())), preferred_element_type=f32)


def dot_nt(a, b):
    return lax.dot_general(a, b, (((1,), (1,)), ((), ())), preferred_element_type=f32)


def split(x):
    high = x.astype(bf16)
    return high, (x - high.astype(f32)).astype(bf16)


def call(kernel, outs, inputs, flops, moved, smem_in=0, smem_out=0, scratch=()):
    return pl.pallas_call(
        kernel,
        out_shape=[jax.ShapeDtypeStruct(s, d) for s, d in outs],
        in_specs=[SMEM] * smem_in + [VMEM] * (len(inputs) - smem_in),
        out_specs=[VMEM] * (len(outs) - smem_out) + [SMEM] * smem_out,
        scratch_shapes=list(scratch),
        cost_estimate=pl.CostEstimate(flops=flops, bytes_accessed=moved, transcendentals=0),
        compiler_params=pltpu.CompilerParams(vmem_limit_bytes=GRANT),
    )(*inputs)


def parts_of(x, size):
    if size & (size - 1):
        return lax.div(x, size), lax.rem(x, size)
    return lax.shift_right_logical(x, size.bit_length() - 1), x & (size - 1)


def same_position(size):
    shape = (size, size)
    return lax.broadcasted_iota(jnp.int32, shape, 0) == lax.broadcasted_iota(jnp.int32, shape, 1)


def weights_kernel(cells, regions, live_ref, cell_ref, weight_ref, report_ref, table_ref, place_ref, flip_ref):
    region = lax.axis_index("region")
    bits = regions.bit_length() - 1
    points, slots = weight_ref.shape[1:]
    rows = cells // LANES + 2
    holder, within = parts_of(cell_ref[...], cells)
    block, low = parts_of(within, LANES)
    outside = holder != region
    named = holder.astype(f32)
    first = jnp.min(jnp.where(outside, named, float(regions))).astype(jnp.int32)
    second = jnp.max(jnp.where(outside, named, -1.0)).astype(jnp.int32)
    first = jnp.where(first == regions, region, first)
    second = jnp.where(second < 0, region, second)
    for j, source in enumerate((first, second)):
        distance = region ^ source
        place = jnp.int32(0)
        flip = jnp.int32(0)
        for k in range(bits):
            bit = (distance >> k) & 1
            place = place + (bit << (bits - 1 - k))
            flip = flip ^ bit
        place_ref[j : j + 1, :] = jnp.full((1, LANES), place, jnp.int32)
        flip_ref[j] = flip
    high = jnp.where(outside, jnp.where(holder == first, rows - 2, rows - 1), block)
    active = lax.broadcasted_iota(jnp.int32, (1, slots), 1) < live_ref[...]
    weights = jnp.where(active, weight_ref[0], 0.0)
    values = jnp.concatenate([weights, weights * report_ref[...]], axis=0)
    low_hot = (lax.broadcasted_iota(jnp.int32, (LANES, slots), 0) == low).astype(f32).astype(bf16)
    chosen = jnp.concatenate(
        [jnp.where(high == row, values, 0.0) for row in range(rows)], axis=0
    )
    first, second = split(chosen)
    total = dot_nt(first, low_hot) + dot_nt(second, low_hot)
    table_ref[...] = total.reshape(rows, 2 * points, LANES)


def pick_kernel(place_ref, near_ref, far_ref, out_ref):
    count = near_ref.shape[0]
    for j in range(2):
        place = jnp.broadcast_to(place_ref[j : j + 1, :], near_ref.shape[1:])
        chosen = jnp.zeros(near_ref.shape[1:], f32)
        for ref, base in ((near_ref, 0), (far_ref, count)):
            for i in range(count):
                chosen = jnp.where(place == base + i, ref[i].astype(f32), chosen)
        out_ref[j] = chosen.astype(bf16)


def anomaly_kernel(offsets, *refs):
    pieces, (anomaly_ref, mean_ref) = refs[:-2], refs[-2:]
    member = lax.axis_index("member")
    rows = pieces[0].shape[0]
    members = rows * len(pieces)
    total = jnp.sum(pieces[0][...].astype(f32), axis=0, keepdims=True)
    for piece in pieces[1:]:
        total = total + jnp.sum(piece[...].astype(f32), axis=0, keepdims=True)
    mean = total / members
    mean_ref[...] = mean
    for offset, piece in zip(offsets, pieces):
        start = pl.multiple_of((member ^ offset) * rows, rows)
        anomaly_ref[pl.ds(start, rows), :] = (piece[...].astype(f32) - mean).astype(bf16)


def products_kernel(chosen, anomaly_ref, mean_ref, table_ref, products_ref, *forcing_ref):
    members, cells = anomaly_ref.shape
    points = table_ref.shape[1] // 2
    chunk = min(cells, 2048)
    forcing = None
    for start in range(0, cells, chunk):
        block = anomaly_ref[:, start : start + chunk]
        blocks = range(start // LANES, (start + chunk) // LANES)
        scaled = []
        for a in chosen:
            weighted = [
                anomaly_ref[:, h * LANES : (h + 1) * LANES]
                * table_ref[h, a : a + 1, :].astype(bf16)
                for h in blocks
            ]
            scaled.append(jnp.concatenate(weighted, axis=1))
        if forcing_ref:
            departures = []
            for h in blocks:
                tile = table_ref[h]
                mean = mean_ref[:, h * LANES : (h + 1) * LANES]
                departures.append(tile[points:, :] - tile[:points, :] * mean)
            departure = jnp.concatenate(departures, axis=1)
            first, second = split(jnp.concatenate([departure, departure], axis=0))
            scaled.append(jnp.concatenate([first, second], axis=0))
        part = dot_nt(jnp.concatenate(scaled, axis=0), block)
        for i in range(len(chosen)):
            rows = part[i * members : (i + 1) * members]
            if start:
                products_ref[i] += rows
            else:
                diagonal = jnp.where(same_position(members), members - 1.0, 0.0)
                products_ref[i] = rows + diagonal
        if forcing_ref:
            rest = part[len(chosen) * members :]
            rest = rest[: 2 * points] + rest[2 * points :]
            forcing = rest if forcing is None else forcing + rest
    if forcing_ref:
        forcing_ref[0][...] = forcing


def cells_kernel(
    row_count, points, anomaly_ref, mean_ref, own_blend, first_blend, second_blend,
    own_ref, first_ref, second_ref, own_mix, first_mix, second_mix, column_ref
):
    member = lax.axis_index("member")
    odd = member & 1
    partner = member ^ 1
    other = member - 1 + 2 * odd
    exists = (other >= 0) & (other < row_count)
    other = jnp.where(exists, other, 0)
    slab = own_ref.shape[0]
    half = slab // 2
    for ref, band in ((own_ref, member), (first_ref, partner)):
        for u in range(2):
            start = pl.multiple_of(band * slab + u * half, half)
            ref[u * half : (u + 1) * half, :] = anomaly_ref[:, pl.ds(start, half)].T
    start = pl.multiple_of(other * slab + (1 - odd) * half, half)
    second_ref[...] = anomaly_ref[:, pl.ds(start, half)].T
    row = mean_ref[:, pl.ds(pl.multiple_of(member * slab, slab), slab)]
    column_ref[...] = jnp.broadcast_to(row, (8, slab)).T
    cell = lax.broadcasted_iota(jnp.int32, (1, slab), 1)
    upper = cell < half
    bases = column_bases(points)
    size = half // len(bases)
    inside = jnp.where(upper, cell, cell - half)
    base = jnp.zeros_like(cell)
    for g in range(1, len(bases)):
        base = base + jnp.where(inside >= g * size, bases[g] - bases[g - 1], 0)

    def columns(blend_ref, band, valid):
        blending = blend_ref[...]
        mixing = blending / jnp.sum(blending, axis=0, keepdims=True)
        tops = [jnp.clip(band - 1 + u, 0, row_count - 2) for u in range(2)]
        step = member - jnp.where(upper, tops[0], tops[1])
        pairs = []
        for c in range(2):
            pair = jnp.where(
                step == 0, mixing[c : c + 1], jnp.where(step == 1, mixing[2 + c : 3 + c], 0.0)
            )
            pairs.append(jnp.where(valid, pair, 0.0))
        rows = [
            jnp.where(base == q, pairs[0], jnp.where(base == q - 1, pairs[1], 0.0))
            for q in range(points)
        ]
        rows = rows + [jnp.zeros_like(rows[0])] * (-points % 8)
        return jnp.concatenate(rows, axis=0)

    own_mix[...] = columns(own_blend, member, True).T
    first_mix[...] = columns(first_blend, partner, True).T
    second = columns(second_blend, other, exists)
    second = jnp.where(odd == 1, second[:, :half], second[:, half:])
    second_mix[...] = second.T


def column_bases(points):
    return [min(max(b - 1 + v, 0), points - 2) for b in range(points) for v in range(2)]


def blended_parts(segments, transforms, points):
    half = segments[0][0].shape[0]
    bases = column_bases(points)
    size = half // len(bases)
    spans = []
    for v in range(points - 1):
        hits = [g for g, b in enumerate(bases) if b == v]
        spans.append((hits[0] * size, (hits[-1] + 1) * size))
    sums = [[None] * (points - 1) for _ in segments]
    for q in range(points):
        where = [v for v in (q - 1, q) if 0 <= v <= points - 2]
        rows = [
            (n, v, cells[spans[v][0] : spans[v][1], :])
            for n, (cells, _) in enumerate(segments)
            for v in where
        ]
        spread = dot_nn(jnp.concatenate([r[2] for r in rows], axis=0), transforms(q))
        at = 0
        for n, v, cells in rows:
            low, high = spans[v]
            term = segments[n][1][low:high, q : q + 1] * spread[at : at + high - low]
            sums[n][v] = term if sums[n][v] is None else sums[n][v] + term
            at += high - low
    return [jnp.concatenate(parts, axis=0) for parts in sums]


def transform_kernel(offsets, flip_ref, *refs):
    count = len(offsets)
    pieces = refs[:count]
    (
        table_ref,
        low_products_ref,
        high_products_ref,
        forcing_ref,
        second_ref,
        second_mix,
        transform_ref,
        to_second_ref,
        margin_ref,
    ) = refs[count:]
    member = lax.axis_index("member")
    rows = pieces[0].shape[1]
    members = rows * count
    last = table_ref.shape[0]
    products_refs = (low_products_ref, high_products_ref)
    half_points = low_products_ref.shape[0]
    points = 2 * half_points
    for offset, piece in zip(offsets, pieces):
        for j in range(2):
            start = pl.multiple_of((member ^ offset ^ flip_ref[j]) * rows, rows)
            margin_ref[pl.ds(start, rows), j * LANES : (j + 1) * LANES] = piece[j]
    values = margin_ref[...].astype(f32)
    mean = jnp.sum(values, axis=0, keepdims=True) / members
    pert = (values - mean).astype(bf16)
    tiles = jnp.concatenate([table_ref[last - 2], table_ref[last - 1]], axis=1)
    departure = tiles[points:, :] - tiles[:points, :] * mean
    first, second = split(jnp.concatenate([departure, departure], axis=0))
    forcing = forcing_ref[...] + dot_nt(first, pert) + dot_nt(second, pert)
    forcing = forcing.T

    def steps(a):
        weighted = pert * tiles[a : a + 1, :].astype(bf16)
        full = products_refs[a // half_points][a % half_points] + dot_nt(weighted, pert)
        yield
        square = jnp.sum(jnp.sum(full * full, axis=0, keepdims=True), axis=1, keepdims=True)
        norm = lax.rsqrt(square)
        h = full * (norm * (1.0 / 3.0))
        h_low = h.astype(bf16)
        yield
        w = h - dot_nn(h_low, h_low)
        w_more = 2.25 * w
        e = h + w_more
        w_low = w.astype(bf16)
        yield
        e = dot_nn(w_more.astype(bf16), h_low + w_low) - e
        e_low = e.astype(bf16)
        yield
        y = 5.0625 * (h + dot_nn(h_low, e_low))
        y_low = y.astype(bf16)
        yield
        g = y + dot_nn(e_low, y_low)
        g_low = g.astype(bf16)
        e = e - g
        yield
        both = dot_nn(jnp.concatenate([y_low, e_low], axis=0), g_low)
        y = 2.25 * (y - both[:members])
        y_low = y.astype(bf16)
        e = e - both[members:]
        e_low = e.astype(bf16)
        yield
        g = y + dot_nn(e_low, y_low)
        g_low = g.astype(bf16)
        e = e - g
        yield
        e = e - dot_nn(g_low, e_low)
        e = e + identity
        scale = 5.0625 * jnp.sqrt(norm)
        inner = jnp.sum(e * forcing[:, a : a + 1], axis=0, keepdims=True)
        outer = jnp.sum(e * inner, axis=1, keepdims=True)
        yield
        transform_ref[a] = (
            scale * scale * outer + (jnp.sqrt(members - 1.0) * scale) * e
        ).astype(bf16)

    identity = jnp.where(same_position(members), 1.0, 0.0)
    running = [steps(a) for a in range(points)]
    tick = 0
    while any(running):
        for a in range(points):
            if running[a] and tick >= LAG * (a // GANG) and next(running[a], True):
                running[a] = None
        tick += 1
    (part,) = blended_parts(
        [(second_ref[...], second_mix[...])], lambda q: transform_ref[q], points
    )
    to_second_ref[...] = part.astype(bf16)


def partner_kernel(transform_ref, first_ref, first_mix, to_first_ref):
    points = transform_ref.shape[0]
    half = first_ref.shape[0] // 2
    segments = [
        (first_ref[0:half, :], first_mix[0:half, :]),
        (first_ref[half:, :], first_mix[half:, :]),
    ]
    parts = blended_parts(segments, lambda q: transform_ref[q], points)
    for u in range(2):
        to_first_ref[u * half : (u + 1) * half, :] = parts[u].astype(bf16)


def own_kernel(transform_ref, own_ref, own_mix, column_ref, out_ref):
    points = transform_ref.shape[0]
    half = own_ref.shape[0] // 2
    segments = [
        (own_ref[0:half, :], own_mix[0:half, :]),
        (own_ref[half:, :], own_mix[half:, :]),
    ]
    parts = blended_parts(segments, lambda q: transform_ref[q], points)
    for u in range(2):
        rows = slice(u * half, (u + 1) * half)
        out_ref[rows, :] = parts[u] + column_ref[rows, 0:1]


def per_device(ensemble, reports, report_count, report_cell, report_weight, blending):
    local_members, cell_count = ensemble.shape
    regions = lax.axis_size("region")
    groups = lax.axis_size("member")
    members = local_members * groups
    points = report_weight.shape[1]
    slots = reports.shape[1]
    slab = cell_count // groups
    half = slab // 2
    devices = regions * groups
    region_bits = regions.bit_length() - 1
    member_bits = groups.bit_length() - 1

    def swap(x, mask):
        return lax.ppermute(x, AXES, [(i, i ^ mask) for i in range(devices)])

    def across(i):
        position = i % groups
        if position in (0, groups - 1):
            return (i + groups * (1 - 2 * (i // groups % 2))) if regions > 1 else i
        return i + (1 if position % 2 else -1)

    def cross(x):
        return lax.ppermute(x, AXES, [(i, across(i)) for i in range(devices)])

    member_masks = [(1 << k) | 1 for k in range(member_bits - 1, 0, -1)] + [1]

    table_rows = cell_count // LANES + 2
    table, places, flips = call(
        functools.partial(weights_kernel, cell_count, regions),
        [
            ((table_rows, 2 * points, LANES), f32),
            ((2, LANES), jnp.int32),
            ((2,), jnp.int32),
        ],
        (report_count[None], report_cell, report_weight, reports),
        4 * table_rows * 2 * points * slots * LANES,
        100000,
        smem_out=1,
    )

    near = ensemble[:, :MARGIN][None]
    for k in range(region_bits - 1, -1, -1):
        far = swap(near, (groups << k) | 1)
        if k:
            near = jnp.concatenate([near, far], axis=0)
    (picked,) = call(
        pick_kernel,
        [((2, local_members, MARGIN), bf16)],
        (places, near, far),
        0,
        100000,
    )
    margins = [picked]
    for step, mask in enumerate(member_masks):
        if step == 0:
            margins = margins + [swap(picked, mask)]
        else:
            joined = swap(jnp.concatenate(margins, axis=0), mask)
            margins = margins + [joined[2 * i : 2 * i + 2] for i in range(len(margins))]

    pieces, offsets = [ensemble], [0]
    for mask in member_masks:
        pieces = pieces + [swap(x, mask) for x in pieces]
        offsets = offsets + [offset ^ mask for offset in offsets]
    partner_blending = swap(blending, 1)
    other_blending = lax.ppermute(
        blending,
        "member",
        [(i, (i + (1 if i % 2 else -1)) % groups) for i in range(groups)],
    )

    anomaly, mean = call(
        functools.partial(anomaly_kernel, tuple(offsets)),
        [((members, cell_count), bf16), ((1, cell_count), f32)],
        tuple(pieces),
        4 * members * cell_count,
        4 * members * cell_count,
    )
    products = []
    for part in range(2):
        chosen = range(part * points // 2, (part + 1) * points // 2)
        outs = [((len(chosen), members, members), f32)]
        products += call(
            functools.partial(products_kernel, tuple(chosen)),
            outs + ([] if part else [((2 * points, members), f32)]),
            (anomaly, mean, table),
            points * members * members * cell_count,
            2 * members * cell_count + 2 * points * members * members,
        )
    low_products, forcing, high_products = products
    padded = points + -points % 8
    own_cells, first_cells, second_cells, own_mix, first_mix, second_mix, column = call(
        functools.partial(cells_kernel, groups, points),
        [
            ((slab, members), bf16),
            ((slab, members), bf16),
            ((half, members), bf16),
            ((slab, padded), f32),
            ((slab, padded), f32),
            ((half, padded), f32),
            ((slab, 8), f32),
        ],
        (anomaly, mean, blending, partner_blending, other_blending),
        3 * slab * members,
        8 * slab * members,
    )
    transform, to_second = call(
        functools.partial(transform_kernel, tuple(offsets)),
        [((points, members, members), bf16), ((half, members), bf16)],
        (flips, *margins, table, low_products, high_products, forcing, second_cells, second_mix),
        2 * 10 * points * members**3,
        8 * points * members * members,
        smem_in=1,
        scratch=[pltpu.VMEM((members, 2 * LANES), bf16)],
    )
    from_other = cross(to_second)
    (to_first,) = call(
        partner_kernel,
        [((slab, members), bf16)],
        (transform, first_cells, first_mix),
        4 * slab * members * members,
        8 * slab * members,
    )
    from_partner = swap(to_first, 1)
    (own,) = call(
        own_kernel,
        [((slab, members), f32)],
        (transform, own_cells, own_mix, column),
        4 * slab * members * members,
        8 * slab * members,
    )
    odd = lax.axis_index("member") % 2
    upper = jnp.where(odd == 0, from_other.astype(f32), 0.0)
    lower = jnp.where(odd == 1, from_other.astype(f32), 0.0)
    total = own + from_partner.astype(f32) + jnp.concatenate([upper, lower], axis=0)
    return total.astype(bf16)


def solution(mesh):
    return jax.shard_map(
        per_device,
        mesh=mesh,
        in_specs=(
            P("member", "region"),
            P("region", None),
            P("region"),
            P("region", None),
            P("region", "member", None),
            P(None, ("region", "member")),
        ),
        out_specs=P(("region", "member"), None),
        check_vma=False,
    )
```

```python
import functools

import jax
import jax.numpy as jnp
from jax import lax
from jax.experimental import pallas as pl
from jax.experimental.pallas import tpu as pltpu
from jax.sharding import PartitionSpec as P


MARGIN = 128
LANES = 128
GRANT = 20 << 20
GANG = 2
LAG = 1
AXES = ("region", "member")

f32 = jnp.float32
bf16 = jnp.bfloat16

VMEM = pl.BlockSpec(memory_space=pltpu.VMEM)
SMEM = pl.BlockSpec(memory_space=pltpu.SMEM)


def dot_nn(a, b):
    return lax.dot_general(a, b, (((1,), (0,)), ((), ())), preferred_element_type=f32)


def dot_nt(a, b):
    return lax.dot_general(a, b, (((1,), (1,)), ((), ())), preferred_element_type=f32)


def split(x):
    high = x.astype(bf16)
    return high, (x - high.astype(f32)).astype(bf16)


def call(kernel, outs, inputs, flops, moved, smem_in=0, smem_out=0, scratch=()):
    return pl.pallas_call(
        kernel,
        out_shape=[jax.ShapeDtypeStruct(s, d) for s, d in outs],
        in_specs=[SMEM] * smem_in + [VMEM] * (len(inputs) - smem_in),
        out_specs=[VMEM] * (len(outs) - smem_out) + [SMEM] * smem_out,
        scratch_shapes=list(scratch),
        cost_estimate=pl.CostEstimate(flops=flops, bytes_accessed=moved, transcendentals=0),
        compiler_params=pltpu.CompilerParams(vmem_limit_bytes=GRANT),
    )(*inputs)


def parts_of(x, size):
    if size & (size - 1):
        return lax.div(x, size), lax.rem(x, size)
    return lax.shift_right_logical(x, size.bit_length() - 1), x & (size - 1)


def same_position(size):
    shape = (size, size)
    return lax.broadcasted_iota(jnp.int32, shape, 0) == lax.broadcasted_iota(jnp.int32, shape, 1)


def extra_rows(row_count):
    pairs = row_count // 2
    return 0 if pairs == 1 else 1 if pairs == 2 else 2


def extra_place(slot, row_count):
    member = lax.axis_index("member")
    pair = member >> 1
    right = jnp.where(pair == 0, 1, 0) if row_count == 4 else jnp.int32(slot)
    row = 2 * pair - 1 + 3 * right
    exists = (row >= 0) & (row < row_count)
    return right, row, exists, (member & 1) == right


def summed(weights, reports, high, low_hot, weight_table, report_table):
    rows, padded, _ = weight_table.shape
    points, slots = weights.shape
    weights = weights.astype(bf16).astype(f32)
    scaled = weights * reports
    scaled_high = scaled.astype(bf16).astype(f32)
    values = jnp.concatenate([weights, scaled_high, scaled - scaled_high], axis=0)
    if -3 * points % 8:
        values = jnp.concatenate([values, jnp.zeros((-3 * points % 8, slots), f32)], axis=0)
    size = values.shape[0]
    chosen = [jnp.where(high == row, values, 0.0) for row in range(rows)]
    total = dot_nt(jnp.concatenate(chosen, axis=0).astype(bf16), low_hot)
    total = total.reshape(rows, size, LANES)
    weight_table[:, 0:points, :] = total[:, 0:points]
    report_table[:, 0:points, :] = total[:, points : 2 * points] + total[:, 2 * points : 3 * points]
    if padded > points:
        empty = jnp.zeros((rows, padded - points, LANES), f32)
        weight_table[:, points:, :] = empty
        report_table[:, points:, :] = empty


def weights_kernel(
    cells, regions, live_ref, cell_ref, weight_ref, report_ref,
    weight_table, report_table, high_ref, low_ref, place_ref, flip_ref
):
    region = lax.axis_index("region")
    bits = regions.bit_length() - 1
    slots = weight_ref.shape[2]
    rows = cells // LANES + 2
    holder, within = parts_of(cell_ref[...], cells)
    block, low = parts_of(within, LANES)
    outside = holder != region
    named = holder.astype(f32)
    first = jnp.min(jnp.where(outside, named, float(regions))).astype(jnp.int32)
    second = jnp.max(jnp.where(outside, named, -1.0)).astype(jnp.int32)
    first = jnp.where(first == regions, region, first)
    second = jnp.where(second < 0, region, second)
    for j, source in enumerate((first, second)):
        distance = region ^ source
        place = jnp.int32(0)
        flip = jnp.int32(0)
        for k in range(bits):
            bit = (distance >> k) & 1
            place = place + (bit << (bits - 1 - k))
            flip = flip ^ bit
        place_ref[j : j + 1, :] = jnp.full((1, LANES), place, jnp.int32)
        flip_ref[j] = flip
    high = jnp.where(outside, jnp.where(holder == first, rows - 2, rows - 1), block)
    active = lax.broadcasted_iota(jnp.int32, (1, slots), 1) < live_ref[...]
    high = jnp.where(active, high, -1)
    low_hot = (lax.broadcasted_iota(jnp.int32, (LANES, slots), 0) == low).astype(f32).astype(bf16)
    high_ref[...] = high
    low_ref[...] = low_hot
    summed(weight_ref[0], report_ref[...], high, low_hot, weight_table, report_table)


def extra_kernel(
    row_count, high_ref, low_ref, report_ref, across_ref, back_ref, weight_table, report_table
):
    odd = lax.axis_index("member") & 1
    points = across_ref.shape[1]
    weights = []
    for slot in range(extra_rows(row_count)):
        _, _, exists, needed = extra_place(slot, row_count)
        wanted = jnp.where(needed, across_ref[0], back_ref[0])
        wanted = jnp.where(odd == 1, wanted[points // 2 :], wanted[: points // 2])
        weights.append(jnp.where(exists, wanted, 0.0))
    weights = jnp.concatenate(weights, axis=0)
    summed(weights, report_ref[...], high_ref[...], low_ref[...], weight_table, report_table)


def pick_kernel(place_ref, near_ref, far_ref, out_ref):
    count = near_ref.shape[0]
    for j in range(2):
        place = jnp.broadcast_to(place_ref[j : j + 1, :], near_ref.shape[1:])
        chosen = jnp.zeros(near_ref.shape[1:], f32)
        for ref, base in ((near_ref, 0), (far_ref, count)):
            for i in range(count):
                chosen = jnp.where(place == base + i, ref[i].astype(f32), chosen)
        out_ref[j] = chosen.astype(bf16)


def anomaly_kernel(offsets, *refs):
    pieces, (anomaly_ref, mean_ref) = refs[:-2], refs[-2:]
    member = lax.axis_index("member")
    rows = pieces[0].shape[0]
    members = rows * len(pieces)
    total = jnp.sum(pieces[0][...].astype(f32), axis=0, keepdims=True)
    for piece in pieces[1:]:
        total = total + jnp.sum(piece[...].astype(f32), axis=0, keepdims=True)
    mean = total / members
    mean_ref[...] = mean
    for offset, piece in zip(offsets, pieces):
        start = pl.multiple_of((member ^ offset) * rows, rows)
        anomaly_ref[pl.ds(start, rows), :] = (piece[...].astype(f32) - mean).astype(bf16)


def products_kernel(chosen, forced, anomaly_ref, mean_ref, *refs):
    tables, (products_ref, forcing_ref) = refs[:-2], refs[-2:]
    members, cells = anomaly_ref.shape
    points = forcing_ref.shape[0]
    chunk = min(cells, 2048)
    for start in range(0, cells, chunk):
        block = anomaly_ref[:, start : start + chunk]
        blocks = range(start // LANES, (start + chunk) // LANES)
        scaled = []
        for t, a in chosen:
            weighted = [
                anomaly_ref[:, h * LANES : (h + 1) * LANES]
                * tables[2 * t][h, a : a + 1, :].astype(bf16)
                for h in blocks
            ]
            scaled.append(jnp.concatenate(weighted, axis=1))
        departures = []
        for h in blocks:
            mean = mean_ref[:, h * LANES : (h + 1) * LANES]
            departures.append(tables[2 * forced + 1][h] - tables[2 * forced][h] * mean)
        scaled += list(split(jnp.concatenate(departures, axis=1)))
        part = dot_nt(jnp.concatenate(scaled, axis=0), block)
        for i in range(len(chosen)):
            rows = part[i * members : (i + 1) * members]
            if start:
                products_ref[i] += rows
            else:
                diagonal = jnp.where(same_position(members), members - 1.0, 0.0)
                products_ref[i] = rows + diagonal
        rest = part[len(chosen) * members :]
        rest = rest[:points] + rest[points:]
        forcing_ref[...] = rest if start == 0 else forcing_ref[...] + rest


def mixing_rows(blend_ref, band, row, valid, row_count, points):
    blending = blend_ref[...]
    slab = blending.shape[1]
    half = slab // 2
    mixing = blending / jnp.sum(blending, axis=0, keepdims=True)
    cell = lax.broadcasted_iota(jnp.int32, (1, slab), 1)
    upper = cell < half
    bases = column_bases(points)
    size = half // len(bases)
    inside = jnp.where(upper, cell, cell - half)
    base = jnp.zeros_like(cell)
    for g in range(1, len(bases)):
        base = base + jnp.where(inside >= g * size, bases[g] - bases[g - 1], 0)
    tops = [jnp.clip(band - 1 + u, 0, row_count - 2) for u in range(2)]
    step = row - jnp.where(upper, tops[0], tops[1])
    pairs = []
    for c in range(2):
        pair = jnp.where(
            step == 0, mixing[c : c + 1], jnp.where(step == 1, mixing[2 + c : 3 + c], 0.0)
        )
        pairs.append(jnp.where(valid, pair, 0.0))
    return [
        jnp.where(base == q, pairs[0], jnp.where(base == q - 1, pairs[1], 0.0))
        for q in range(points)
    ]


def stacked(rows):
    rows = rows + [jnp.zeros_like(rows[0])] * (-len(rows) % 8)
    return jnp.concatenate(rows, axis=0).T


def band_cells(partner, row_count, points, anomaly_ref, blend_ref, cells_ref, mix_ref, extra_refs):
    member = lax.axis_index("member")
    band = member ^ 1 if partner else member
    slab = cells_ref.shape[0]
    half = slab // 2
    for u in range(2):
        start = pl.multiple_of(band * slab + u * half, half)
        cells_ref[u * half : (u + 1) * half, :] = anomaly_ref[:, pl.ds(start, half)].T
    mix_ref[...] = stacked(mixing_rows(blend_ref, band, member, True, row_count, points))
    few = points // 2
    for slot, ref in enumerate(extra_refs):
        right, row, exists, needed = extra_place(slot, row_count)
        valid = exists & (needed != partner)
        rows = mixing_rows(blend_ref, band, row, valid, row_count, points)
        rows = [jnp.where(right == 1, x[:, half:], x[:, :half]) for x in rows]
        odd = (member & 1) == 1
        ref[...] = stacked([jnp.where(odd, rows[few + j], rows[j]) for j in range(few)])


def partner_cells_kernel(row_count, points, anomaly_ref, blend_ref, cells_ref, mix_ref, *extra_refs):
    band_cells(True, row_count, points, anomaly_ref, blend_ref, cells_ref, mix_ref, extra_refs)


def blended_band(row_count, points, transform_ref, cells_ref, mix_ref, extra_refs, sum_ref):
    half = cells_ref.shape[0] // 2
    halves = [slice(u * half, (u + 1) * half) for u in range(2)]
    parts = blended_parts(
        [(cells_ref[rows, :], mix_ref[rows, :]) for rows in halves],
        lambda q: transform_ref[q],
        points,
    )
    for rows, part in zip(halves, parts):
        sum_ref[rows, :] += part
    few = points // 2
    for slot, ref in enumerate(extra_refs):
        right = extra_place(slot, row_count)[0]
        rows = pl.ds(pl.multiple_of(right * half, half), half)
        cells = cells_ref[rows, :]
        part = None
        for j in range(few):
            term = ref[:, j : j + 1] * dot_nn(cells, transform_ref[points + slot * few + j])
            part = term if part is None else part + term
        sum_ref[rows, :] += part


def column_bases(points):
    return [min(max(b - 1 + v, 0), points - 2) for b in range(points) for v in range(2)]


def blended_parts(segments, transforms, points):
    half = segments[0][0].shape[0]
    bases = column_bases(points)
    size = half // len(bases)
    spans = []
    for v in range(points - 1):
        hits = [g for g, b in enumerate(bases) if b == v]
        spans.append((hits[0] * size, (hits[-1] + 1) * size))
    sums = [[None] * (points - 1) for _ in segments]
    for q in range(points):
        where = [v for v in (q - 1, q) if 0 <= v <= points - 2]
        rows = [
            (n, v, cells[spans[v][0] : spans[v][1], :])
            for n, (cells, _) in enumerate(segments)
            for v in where
        ]
        spread = dot_nn(jnp.concatenate([r[2] for r in rows], axis=0), transforms(q))
        at = 0
        for n, v, cells in rows:
            low, high = spans[v]
            term = segments[n][1][low:high, q : q + 1] * spread[at : at + high - low]
            sums[n][v] = term if sums[n][v] is None else sums[n][v] + term
            at += high - low
    return [jnp.concatenate(parts, axis=0) for parts in sums]


def transform_kernel(offsets, row_count, points, flip_ref, *refs):
    count = len(offsets)
    kinds = 2 if extra_rows(row_count) else 1
    pieces, tables, refs = refs[:count], refs[count : count + 2 * kinds], refs[count + 2 * kinds :]
    products_refs, forcing_refs, refs = refs[:2], refs[2 : 2 + kinds], refs[2 + kinds :]
    cells_ref, mix_ref, *extra_refs, transform_ref, out_ref, margin_ref, sum_ref = refs
    member = lax.axis_index("member")
    rows = pieces[0].shape[1]
    members = rows * count
    last = tables[0].shape[0]
    half_points = products_refs[0].shape[0]
    all_points = 2 * half_points
    for offset, piece in zip(offsets, pieces):
        for j in range(2):
            start = pl.multiple_of((member ^ offset ^ flip_ref[j]) * rows, rows)
            margin_ref[pl.ds(start, rows), j * LANES : (j + 1) * LANES] = piece[j]
    values = margin_ref[...].astype(f32)
    mean = jnp.sum(values, axis=0, keepdims=True) / members
    pert = (values - mean).astype(bf16)
    tiles, departures = [], []
    for kind in range(kinds):
        weights, reports = (
            jnp.concatenate([table[last - 2], table[last - 1]], axis=1)
            for table in tables[2 * kind : 2 * kind + 2]
        )
        tiles.append(weights)
        departures += list(split(reports - weights * mean))
    rest = dot_nt(jnp.concatenate(departures, axis=0), pert)
    forcings = []
    for kind in range(kinds):
        size = tiles[kind].shape[0]
        part = rest[:size] + rest[size : 2 * size]
        rest = rest[2 * size :]
        forcings.append((forcing_refs[kind][...] + part).T)

    def steps(a):
        kind, place = (0, a) if a < points else (1, a - points)
        weighted = pert * tiles[kind][place : place + 1, :].astype(bf16)
        full = products_refs[a // half_points][a % half_points] + dot_nt(weighted, pert)
        full_low = full.astype(bf16)
        yield
        square = jnp.sum(jnp.sum(full * full, axis=0, keepdims=True), axis=1, keepdims=True)
        norm = lax.rsqrt(square)
        matrix = full * norm
        low = matrix.astype(bf16)
        squared = dot_nn(full_low, full_low) * (norm * norm)
        squared_low = squared.astype(bf16)
        e = 0.75 * squared - (13 / 12) * matrix
        yield
        e = e + dot_nn(squared_low, (1 / 36) * squared_low - 0.25 * low)
        e_low = e.astype(bf16)
        yield
        y = matrix + dot_nn(low, e_low)
        y_low = y.astype(bf16)
        yield
        p = y + dot_nn(y_low, e_low)
        p_low = p.astype(bf16)
        yield
        squared = dot_nn(p_low, p_low)
        squared_low = squared.astype(bf16)
        f = (0.75 * 5.0625**2) * squared - (13 / 12 * 5.0625) * p
        yield
        f = f + dot_nn(
            squared_low, (5.0625**4 / 36) * squared_low - (0.25 * 5.0625**3) * p_low
        )
        e = e + f
        yield
        e = e + dot_nn(e_low, f.astype(bf16)) + identity
        scale = 5.0625 * jnp.sqrt(norm)
        inner = jnp.sum(e * forcings[kind][:, place : place + 1], axis=0, keepdims=True)
        outer = jnp.sum(e * inner, axis=1, keepdims=True)
        yield
        transform_ref[a] = (
            scale * scale * outer + (jnp.sqrt(members - 1.0) * scale) * e
        ).astype(bf16)

    identity = jnp.where(same_position(members), 1.0, 0.0)
    running = [steps(a) for a in range(all_points)]
    tick = 0
    while any(running):
        for a in range(all_points):
            if running[a] and tick >= LAG * (a // GANG) and next(running[a], True):
                running[a] = None
        tick += 1
    sum_ref[...] = jnp.zeros(sum_ref.shape, f32)
    blended_band(row_count, points, transform_ref, cells_ref, mix_ref, extra_refs, sum_ref)
    out_ref[...] = sum_ref[...].astype(bf16)


def own_kernel(
    row_count, points, transform_ref, anomaly_ref, mean_ref, blend_ref, out_ref,
    cells_ref, mix_ref, *extra_refs
):
    member = lax.axis_index("member")
    slab = out_ref.shape[0]
    band_cells(False, row_count, points, anomaly_ref, blend_ref, cells_ref, mix_ref, extra_refs)
    row = mean_ref[:, pl.ds(pl.multiple_of(member * slab, slab), slab)]
    column = jnp.broadcast_to(row, (8, slab)).T
    out_ref[...] = jnp.broadcast_to(column[:, 0:1], out_ref.shape)
    blended_band(row_count, points, transform_ref, cells_ref, mix_ref, extra_refs, out_ref)


def per_device(ensemble, reports, report_count, report_cell, report_weight, blending):
    local_members, cell_count = ensemble.shape
    regions = lax.axis_size("region")
    groups = lax.axis_size("member")
    members = local_members * groups
    points = report_weight.shape[1]
    slots = reports.shape[1]
    slab = cell_count // groups
    half = slab // 2
    devices = regions * groups
    region_bits = regions.bit_length() - 1
    member_bits = groups.bit_length() - 1

    def swap(x, mask):
        return lax.ppermute(x, AXES, [(i, i ^ mask) for i in range(devices)])

    member_masks = [(1 << k) | 1 for k in range(member_bits - 1, 0, -1)] + [1]

    table_rows = cell_count // LANES + 2
    extra_count = extra_rows(groups)
    few = points // 2
    all_points = points + extra_count * few

    def tables_of(count):
        return [((table_rows, count + -count % 8, LANES), f32)] * 2

    *own_tables, highs, lows, places, flips = call(
        functools.partial(weights_kernel, cell_count, regions),
        [
            *tables_of(points),
            ((1, slots), jnp.int32),
            ((LANES, slots), bf16),
            ((2, LANES), jnp.int32),
            ((2,), jnp.int32),
        ],
        (report_count[None], report_cell, report_weight, reports),
        6 * table_rows * points * slots * LANES,
        100000,
        smem_out=1,
    )
    tables = own_tables
    if extra_count:
        ring = [(i, (i + (1 if i % 2 else -1)) % groups) for i in range(groups)]
        across = lax.ppermute(report_weight, "member", ring)
        back = swap(across, 1)
        extra_tables = call(
            functools.partial(extra_kernel, groups),
            tables_of(extra_count * few),
            (highs, lows, reports, across, back),
            6 * table_rows * extra_count * few * slots * LANES,
            100000,
        )
        tables = [*own_tables, *extra_tables]

    near = ensemble[:, :MARGIN][None]
    for k in range(region_bits - 1, -1, -1):
        far = swap(near, (groups << k) | 1)
        if k:
            near = jnp.concatenate([near, far], axis=0)
    (picked,) = call(
        pick_kernel,
        [((2, local_members, MARGIN), bf16)],
        (places, near, far),
        0,
        100000,
    )
    margins = [picked]
    for step, mask in enumerate(member_masks):
        if step == 0:
            margins = margins + [swap(picked, mask)]
        else:
            joined = swap(jnp.concatenate(margins, axis=0), mask)
            margins = margins + [joined[2 * i : 2 * i + 2] for i in range(len(margins))]

    pieces, offsets = [ensemble], [0]
    for mask in member_masks:
        pieces = pieces + [swap(x, mask) for x in pieces]
        offsets = offsets + [offset ^ mask for offset in offsets]
    partner_blending = swap(blending, 1)

    anomaly, mean = call(
        functools.partial(anomaly_kernel, tuple(offsets)),
        [((members, cell_count), bf16), ((1, cell_count), f32)],
        tuple(pieces),
        4 * members * cell_count,
        4 * members * cell_count,
    )
    items = [(0, a) for a in range(points)] + [(1, a) for a in range(all_points - points)]
    share = all_points // 2
    products, forcings = [], []
    for part in range(2):
        chosen = tuple(items[part * share : (part + 1) * share])
        forced = part if extra_count else 0
        used = tables if part else own_tables
        product, forcing = call(
            functools.partial(products_kernel, chosen, forced),
            [((share, members, members), f32), ((used[2 * forced].shape[1], members), f32)],
            (anomaly, mean, *used),
            2 * share * members * members * cell_count,
            2 * members * cell_count + 4 * share * members * members,
        )
        products.append(product)
        forcings.append(forcing)
    forcings = forcings if extra_count else forcings[:1]
    band = [
        ((slab, members), bf16),
        ((slab, points + -points % 8), f32),
        *[((half, few + -few % 8), f32)] * extra_count,
    ]
    partner_band = call(
        functools.partial(partner_cells_kernel, groups, points),
        band,
        (anomaly, partner_blending),
        3 * slab * members,
        4 * slab * members,
    )
    transform, to_partner = call(
        functools.partial(transform_kernel, tuple(offsets), groups, points),
        [((all_points, members, members), bf16), ((slab, members), bf16)],
        (
            flips,
            *margins,
            *tables,
            *products,
            *forcings,
            *partner_band,
        ),
        2 * 8 * all_points * members**3,
        8 * all_points * members * members,
        smem_in=1,
        scratch=[
            pltpu.VMEM((members, 2 * LANES), bf16),
            pltpu.VMEM((slab, members), f32),
        ],
    )
    from_partner = swap(to_partner, 1)
    (own,) = call(
        functools.partial(own_kernel, groups, points),
        [((slab, members), f32)],
        (transform, anomaly, mean, blending),
        4 * slab * members * members,
        8 * slab * members,
        scratch=[pltpu.VMEM(*x) for x in band],
    )
    return (own + from_partner.astype(f32)).astype(bf16)


def solution(mesh):
    return jax.shard_map(
        per_device,
        mesh=mesh,
        in_specs=(
            P("member", "region"),
            P("region", None),
            P("region"),
            P("region", None),
            P("region", "member", None),
            P(None, ("region", "member")),
        ),
        out_specs=P(("region", "member"), None),
        check_vma=False,
    )
```
